32 devices in a mesh: grp: 4 (over z), gz: 8 (over y, x, core).
Axes of the slice: x: 2, y: 2, z: 4, core: 2. Of those that a mesh axis runs over, the one named last changes fastest.
Arguments:
- load: float32 [3, 256, 64, 128], P(None, ('grp', 'gz')), may hold values from -128 to 128
- phases: int32 [256, 64, 128], P(('grp', 'gz')), may hold values from 0 to 3
- clamp: int32 [64, 128], replicated, may hold values 0 or 1
- phase_moduli: float32 [4], replicated, may hold values from 0.05 to 1
Outputs:
- displacement: float32 [3, 256, 64, 128], P(None, ('grp', 'gz'))
- residual: float32 [3, 256, 64, 128], P(None, ('grp', 'gz'))
The draws below stay inside these ranges and needn't reach their ends.
All inputs are finite; a program needn't handle non-finite values.
Results may differ from the reference program's by a relative error of at most 0.0003.
Values sent between devices are 32-bit elements; how exact they have to be, the bound alone decides.
A program may use at most 128 MiB of HBM per device.

```python
import math
import jax
import jax.numpy as jnp
import numpy as np
from jax import lax

NX = 128
NY = 64
PHASES = 4
COARSEN = 8
CHEB = 4
ITERS = 2
NZ = 256
COARSE_Y = 8
COARSE_X = 16
GROUP_COARSE = 8
N_GRP = 4


def draw_load(key, part):
    keys = jax.random.split(key, 2)
    shape = (3, NZ, NY, NX)
    base = jnp.clip(jax.random.normal(keys[0], shape, jnp.float32), -4.0, 4.0)
    rough = jnp.exp(jax.random.uniform(keys[1], shape, jnp.float32, -0.7, 0.7))
    depth = jnp.arange(NZ, dtype=jnp.float32)[None, :, None, None] / float(max(NZ - 1, 1))
    rising = jnp.exp(depth * math.log(3.0))
    return 0.5 * base * rough * rising


def place_ends(result, stream_key, least, largest):
    index_at = [jax.random.randint(jax.random.fold_in(stream_key, axis), (), 0, length) for axis, length in enumerate(result.shape)]
    main_axis = result.shape.index(max(result.shape))
    beside = index_at[:main_axis] + [(index_at[main_axis] + 1) % result.shape[main_axis]] + index_at[main_axis + 1:]
    return result.at[tuple(index_at)].set(least).at[tuple(beside)].set(largest)


def setup_inputs(seed: int = 0) -> dict:
    arg_keys = jax.random.split(jax.random.key(seed), 5)
    return {
        "load": draw_load(jax.random.fold_in(arg_keys[4], 71), 0),
        "phases": place_ends(jax.random.randint(arg_keys[1], (NZ, NY, NX), 0, PHASES), jax.random.fold_in(arg_keys[1], 1), 0, PHASES - 1).astype(jnp.int32),
        "clamp": place_ends((jax.random.randint(arg_keys[2], (NY, NX), 0, 4) < 3).astype(jnp.int32), jax.random.fold_in(arg_keys[2], 1), 0, 1),
        "phase_moduli": jnp.clip(jnp.exp(jax.random.uniform(arg_keys[3], (PHASES,), jnp.float32, math.log(0.05), math.log(1.0))), 0.05, 1.0),
    }


CORNER_OFFSETS = [(along_z, along_y, along_x) for along_z in (0, 1) for along_y in (0, 1) for along_x in (0, 1)]

def element_matrix():
    poisson = 0.3
    lame_first = poisson / ((1.0 + poisson) * (1.0 - 2.0 * poisson))
    shear = 1.0 / (2.0 * (1.0 + poisson))
    elastic = np.zeros((6, 6))
    elastic[:3, :3] = lame_first
    for axis_one in range(3):
        elastic[axis_one, axis_one] = lame_first + 2.0 * shear
        elastic[axis_one + 3, axis_one + 3] = shear
    points = [0.5 - 0.5 / math.sqrt(3.0), 0.5 + 0.5 / math.sqrt(3.0)]
    pairs = [(0, 1), (1, 2), (0, 2)]
    matrix = np.zeros((24, 24))
    for first_point in points:
        for second_point in points:
            for third_point in points:
                spot = (first_point, second_point, third_point)
                strain = np.zeros((6, 24))
                for corner, offset in enumerate(CORNER_OFFSETS):
                    values = [spot[axis_one] if offset[axis_one] else 1.0 - spot[axis_one] for axis_one in range(3)]
                    slopes = [1.0 if offset[axis_one] else -1.0 for axis_one in range(3)]
                    slants = []
                    for axis_one in range(3):
                        others = [values[axis_two] for axis_two in range(3) if axis_two != axis_one]
                        slants.append(slopes[axis_one] * others[0] * others[1])
                        strain[axis_one, 3 * corner + axis_one] = slants[axis_one]
                    for position, pair in enumerate(pairs):
                        strain[3 + position, 3 * corner + pair[0]] = slants[pair[1]]
                        strain[3 + position, 3 * corner + pair[1]] = slants[pair[0]]
                matrix = matrix + 0.125 * (strain.T @ elastic @ strain)
    return matrix

def spectral_bound(numbers):
    diagonal_part = np.array([numbers[index, index] for index in range(numbers.shape[0])])
    return float(np.max(np.sum(np.abs(numbers), axis=1) / diagonal_part))

def element_forces(extended, moduli, matrix):
    layers = moduli.shape[0]
    width = min(4, layers)
    blocks = (layers + width - 1) // width
    extra = blocks * width - layers
    plane = tuple(extended.shape[2:])
    if extra > 0:
        moduli = jnp.concatenate([moduli, jnp.zeros((extra,) + tuple(moduli.shape[1:]), moduli.dtype)], 0)
        extended = jnp.concatenate([extended, jnp.zeros((3, extra) + plane, extended.dtype)], 1)

    def add_block(total, index):
        start = index * width
        nodes = lax.dynamic_slice_in_dim(extended, start, width + 1, 1)
        weights = lax.dynamic_slice_in_dim(moduli, start, width, 0)
        gathered = jnp.stack([jnp.roll(nodes[:, along_z:along_z + width], (-along_y, -along_x), (2, 3)) for along_z, along_y, along_x in CORNER_OFFSETS], 0)
        gathered = gathered.reshape((24, width) + plane)
        forces = jnp.einsum('ij,jzyx->izyx', matrix, gathered, precision=lax.Precision.HIGHEST) * weights
        forces = forces.reshape((8, 3, width) + plane)
        update = jnp.zeros((3, width + 1) + plane, jnp.float32)
        for corner, offset in enumerate(CORNER_OFFSETS):
            update = update.at[:, offset[0]:offset[0] + width].add(jnp.roll(forces[corner], (offset[1], offset[2]), (2, 3)))
        current = lax.dynamic_slice_in_dim(total, start, width + 1, 1)
        return (lax.dynamic_update_slice_in_dim(total, current + update, start, 1), None)
    initial = jnp.zeros(extended.shape, jnp.float32)
    total, unused = lax.scan(add_block, initial, jnp.arange(blocks, dtype=jnp.int32))
    return total[:, :layers + 1]

def node_diagonal(lower, moduli, matrix):
    layers = moduli.shape[0]
    extended = jnp.concatenate([lower, moduli], 0)
    entries = jnp.diagonal(matrix).reshape(8, 3)
    total = jnp.zeros((3,) + tuple(moduli.shape), jnp.float32)
    for corner, offset in enumerate(CORNER_OFFSETS):
        shifted = jnp.roll(extended[1 - offset[0]:1 - offset[0] + layers], (offset[1], offset[2]), (1, 2))
        total = total + entries[corner][:, None, None, None] * shifted[None]
    return total

def chebyshev(rhs, coarse_apply, coarse_inverse, bound, sweeps):
    top = bound
    bottom = bound / 20.0
    center = 0.5 * (top + bottom)
    radius = 0.5 * (top - bottom)
    sigma = center / radius
    rho = 1.0 / sigma
    update = coarse_inverse * rhs / center
    correction = update
    remainder = rhs
    for sweep in range(sweeps - 1):
        remainder = remainder - coarse_apply(update)
        rho_next = 1.0 / (2.0 * sigma - rho)
        update = rho_next * rho * update + 2.0 * rho_next / radius * coarse_inverse * remainder
        correction = correction + update
        rho = rho_next
    return correction

def restrict(field, factor):
    comps, layers, height, breadth = field.shape
    return field.reshape(comps, layers // factor, factor, height // factor, factor, breadth // factor, factor).sum((2, 4, 6))

def prolong(coarse, factor):
    comps, layers, height, breadth = coarse.shape
    expanded = jnp.broadcast_to(coarse[:, :, None, :, None, :, None], (comps, layers, factor, height, factor, breadth, factor))
    return expanded.reshape(comps, layers * factor, height * factor, breadth * factor)

def reference(load, phases, clamp, phase_moduli):
    numbers = element_matrix()
    matrix = jnp.asarray(numbers, jnp.float32)
    bound = spectral_bound(numbers)
    omega = 1.2 / bound
    depth = jnp.arange(NZ, dtype=jnp.int32)[:, None, None]
    rows_at = jnp.arange(NY, dtype=jnp.int32)[None, :, None]
    columns_at = jnp.arange(NX, dtype=jnp.int32)[None, None, :]
    picked = jnp.zeros((NZ, NY, NX), jnp.float32)
    for phase in range(PHASES):
        picked = picked + jnp.where(phases == phase, phase_moduli[phase], jnp.float32(0.0))
    outside = (depth == NZ - 1) | (rows_at == NY - 1) | (columns_at == NX - 1)
    moduli = jnp.where(outside, jnp.float32(0.0), picked)
    free = jnp.where((depth == 0) & (clamp[None] == 1), 0.0, 1.0).astype(jnp.float32)
    edge = jnp.zeros((1, NY, NX), jnp.float32)
    inverse = 1.0 / (free * node_diagonal(edge, moduli, matrix) + 1.0 - free)
    top_layer = jnp.zeros((3, 1, NY, NX), jnp.float32)

    def operator(field):
        total = element_forces(jnp.concatenate([free * field, top_layer], 1), moduli, matrix)
        return free * total[:, :-1] + (1.0 - free) * field
    factor = COARSEN
    block_mean = moduli.reshape(NZ // factor, factor, COARSE_Y, factor, COARSE_X, factor).mean((1, 3, 5))
    coarse_depth = jnp.arange(NZ // factor, dtype=jnp.int32)[:, None, None]
    coarse_rows = jnp.arange(COARSE_Y, dtype=jnp.int32)[None, :, None]
    coarse_columns = jnp.arange(COARSE_X, dtype=jnp.int32)[None, None, :]
    coarse_edge = (coarse_depth % GROUP_COARSE == GROUP_COARSE - 1) | (coarse_rows == COARSE_Y - 1) | (coarse_columns == COARSE_X - 1)
    group_moduli = jnp.where(coarse_edge, jnp.float32(0.0), block_mean).reshape(N_GRP, GROUP_COARSE, COARSE_Y, COARSE_X)
    coarse_matrix = factor * matrix
    coarse_bottom = jnp.zeros((1, COARSE_Y, COARSE_X), jnp.float32)
    coarse_top = jnp.zeros((3, 1, COARSE_Y, COARSE_X), jnp.float32)
    coarse_inverse = jax.vmap(lambda weights: 1.0 / node_diagonal(coarse_bottom, weights, coarse_matrix))(group_moduli)

    def solve_one(rhs, weights, group_inverse):

        def coarse_apply(field):
            return element_forces(jnp.concatenate([field, coarse_top], 1), weights, coarse_matrix)[:, :-1]
        return chebyshev(rhs, coarse_apply, group_inverse, bound, CHEB)

    def precondition(current):
        first = omega * current * inverse
        defect = current - operator(first)
        restricted = restrict(defect, factor).reshape(3, N_GRP, GROUP_COARSE, COARSE_Y, COARSE_X)
        solved = jax.vmap(solve_one)(jnp.moveaxis(restricted, 1, 0), group_moduli, coarse_inverse)
        own = jnp.moveaxis(solved, 0, 1).reshape(3, NZ // factor, COARSE_Y, COARSE_X)
        second = first + free * prolong(own, factor)
        return second + omega * (current - operator(second)) * inverse
    rhs = free * load
    displacement = jnp.zeros_like(rhs)
    residual = rhs
    preconditioned = precondition(residual)
    direction = preconditioned
    gamma = jnp.sum(residual * preconditioned)
    for step in range(ITERS):
        image = operator(direction)
        alpha = gamma / jnp.sum(direction * image)
        displacement = displacement + alpha * direction
        residual = residual - alpha * image
        if step + 1 < ITERS:
            preconditioned = precondition(residual)
            following = jnp.sum(residual * preconditioned)
            direction = preconditioned + following / gamma * direction
            gamma = following
    return (displacement, residual)
```

```python
import functools
import math

import jax
import jax.numpy as jnp
import numpy as np
from jax import lax
from jax.experimental import pallas as pl
from jax.experimental.pallas import tpu as pltpu
from jax.sharding import PartitionSpec as P

PHASES = 4
COARSEN = 8
CHEB = 4
ITERS = 2
HALO = 2
MESH = pl.DeviceIdType.MESH

POISSON = 0.3
LAME = POISSON / ((1.0 + POISSON) * (1.0 - 2.0 * POISSON))
SHEAR = 1.0 / (2.0 * (1.0 + POISSON))


CORNER_OFFSETS = [
    (along_z, along_y, along_x) for along_z in (0, 1) for along_y in (0, 1) for along_x in (0, 1)
]


def element_matrix():
    elastic = np.zeros((6, 6))
    elastic[:3, :3] = LAME
    for axis_one in range(3):
        elastic[axis_one, axis_one] = LAME + 2.0 * SHEAR
        elastic[axis_one + 3, axis_one + 3] = SHEAR
    points = [0.5 - 0.5 / math.sqrt(3.0), 0.5 + 0.5 / math.sqrt(3.0)]
    pairs = [(0, 1), (1, 2), (0, 2)]
    matrix = np.zeros((24, 24))
    for first_point in points:
        for second_point in points:
            for third_point in points:
                spot = (first_point, second_point, third_point)
                strain = np.zeros((6, 24))
                for corner, offset in enumerate(CORNER_OFFSETS):
                    values = [
                        spot[axis_one] if offset[axis_one] else 1.0 - spot[axis_one]
                        for axis_one in range(3)
                    ]
                    slopes = [1.0 if offset[axis_one] else -1.0 for axis_one in range(3)]
                    slants = []
                    for axis_one in range(3):
                        others = [values[axis_two] for axis_two in range(3) if axis_two != axis_one]
                        slants.append(slopes[axis_one] * others[0] * others[1])
                        strain[axis_one, 3 * corner + axis_one] = slants[axis_one]
                    for position, pair in enumerate(pairs):
                        strain[3 + position, 3 * corner + pair[0]] = slants[pair[1]]
                        strain[3 + position, 3 * corner + pair[1]] = slants[pair[0]]
                matrix = matrix + 0.125 * (strain.T @ elastic @ strain)
    return matrix


def spectral_bound(numbers):
    diagonal_part = np.array([numbers[index, index] for index in range(numbers.shape[0])])
    return float(np.max(np.sum(np.abs(numbers), axis=1) / diagonal_part))


def voxel_forces(below, above, mod, scale):
    one, two, three = scale / 16.0, scale / 48.0, scale / 144.0
    u = []
    for k in range(3):
        modes = {}
        for b in (0, 1):
            for c in (0, 1):
                if b or c:
                    modes[(0, b, c)] = below[k][b][c] + above[k][b][c]
                modes[(1, b, c)] = above[k][b][c] - below[k][b][c]
        u.append(modes)
    unit = [(1, 0, 0), (0, 1, 0), (0, 0, 1)]

    def pair(i, j):
        return tuple(unit[i][d] + unit[j][d] for d in range(3))

    f = [{}, {}, {}]
    trace = (mod * (one * LAME)) * (u[0][unit[0]] + u[1][unit[1]] + u[2][unit[2]])
    stretch = mod * (2.0 * one * SHEAR)
    slide = mod * (one * SHEAR)
    for k in range(3):
        f[k][unit[k]] = trace + stretch * u[k][unit[k]]
    for i, j in ((0, 1), (1, 2), (0, 2)):
        shear = slide * (u[i][unit[j]] + u[j][unit[i]])
        f[i][unit[j]] = shear
        f[j][unit[i]] = shear
    same = mod * (two * (LAME + 3.0 * SHEAR))
    cross = mod * (two * LAME)
    for k in range(3):
        for m in range(3):
            if m != k:
                j = 3 - k - m
                f[k][pair(k, m)] = same * u[k][pair(k, m)] + cross * u[j][pair(j, m)]
    twist = mod * (two * SHEAR)
    total = u[0][pair(1, 2)] + u[1][pair(0, 2)] + u[2][pair(0, 1)]
    for k in range(3):
        i, j = [d for d in range(3) if d != k]
        f[k][pair(i, j)] = twist * (u[k][pair(i, j)] + total)
    warp = mod * (three * (LAME + 4.0 * SHEAR))
    for k in range(3):
        f[k][(1, 1, 1)] = warp * u[k][(1, 1, 1)]
    low = [[[None, None], [None, None]] for k in range(3)]
    high = [[[None, None], [None, None]] for k in range(3)]
    for k in range(3):
        for b in (0, 1):
            for c in (0, 1):
                if b or c:
                    low[k][b][c] = f[k][(0, b, c)] - f[k][(1, b, c)]
                    high[k][b][c] = f[k][(0, b, c)] + f[k][(1, b, c)]
                else:
                    low[k][b][c] = -f[k][(1, b, c)]
                    high[k][b][c] = f[k][(1, b, c)]
    return low, high


def plane_modes(value, ahead_y, ahead_x):
    shifted = ahead_x(value)
    rows = [value + shifted, shifted - value]
    out = [[None, None], [None, None]]
    for c in (0, 1):
        up = ahead_y(rows[c])
        out[0][c] = rows[c] + up
        out[1][c] = up - rows[c]
    return out


def plane_forces(force, behind_y, behind_x):
    rows = [
        (force[0][c] - force[1][c]) + behind_y(force[0][c] + force[1][c]) for c in (0, 1)
    ]
    return (rows[0] - rows[1]) + behind_x(rows[0] + rows[1])


def kernel(
    groups,
    members,
    load,
    phases,
    clamp,
    phase_moduli,
    out_u,
    out_r,
    R,
    S,
    W,
    MOD,
    PH,
    FREE,
    PRO,
    FWD,
    FSUM,
    CARRY,
    ACC,
    STAGE,
    GAT,
    DOT,
    DSUM,
    DOTG,
    halo_send,
    halo_recv,
    gat_send,
    gat_recv,
    cross_send,
    cross_recv,
    dot_send,
    dot_recv,
    dotg_send,
    dotg_recv,
):
    numbers = element_matrix()
    entry = float(numbers[0, 0])
    bound = spectral_bound(numbers)
    omega = 1.2 / bound
    _, layers, height, breadth = load.shape
    coarse_height = height // COARSEN
    coarse_breadth = breadth // COARSEN
    grp = lax.axis_index("grp")
    me = lax.axis_index("gz")
    tile = grp * members + me
    tiles = groups * members
    has_below = tile > 0
    has_above = tile < tiles - 1

    GAT[...] = jnp.zeros(GAT.shape, jnp.float32)
    barrier = pltpu.get_barrier_semaphore()

    def greet(o, unused):
        other = lax.rem(tile + o, tiles)
        pl.semaphore_signal(
            barrier,
            inc=1,
            device_id=(other // members, lax.rem(other, members)),
            device_id_type=MESH,
        )
        return unused

    lax.fori_loop(1, tiles, greet, 0)

    rows_at = lax.broadcasted_iota(jnp.int32, (height, breadth), 0)
    columns_at = lax.broadcasted_iota(jnp.int32, (height, breadth), 1)
    inside = (rows_at < height - 1) & (columns_at < breadth - 1)

    def moduli_of(labels, depth):
        picked = jnp.zeros((height, breadth), jnp.float32)
        for phase in range(PHASES):
            picked = jnp.where(labels == phase, phase_moduli[phase], picked)
        keep = jnp.where((depth >= 0) & (depth < tiles * layers - 1), 1.0, 0.0)
        return jnp.where(inside, picked, 0.0) * keep

    first_depth = tile * layers
    bottom = jnp.where(tile == 0, 1.0, 0.0)
    held = jnp.where(clamp[...] == 1, 1.0, 0.0) * bottom
    FREE[0] = 1.0 - held
    FREE[1] = jnp.ones((height, breadth), jnp.float32)

    ACC[0] = jnp.zeros((height, breadth), jnp.float32)

    def own_layer(n, unused):
        mod = moduli_of(phases[n], first_depth + n)
        MOD[n + 3] = mod
        ACC[0] = ACC[0] + mod
        free = FREE[jnp.where(n == 0, 0, 1)]
        for k in range(3):
            R[0, k, n + HALO] = free * load[k, n]
        return unused

    lax.fori_loop(0, layers, own_layer, 0)

    @pl.when(tile == 0)
    def _():
        PH[0:3] = jnp.zeros((3, height, breadth), jnp.int32)
        for it in range(2):
            R[it, :, 0:HALO] = jnp.zeros((3, HALO, height, breadth), jnp.float32)

    @pl.when(tile == tiles - 1)
    def _():
        PH[3:5] = jnp.zeros((2, height, breadth), jnp.int32)
        for it in range(2):
            R[it, :, layers + HALO :] = jnp.zeros((3, HALO, height, breadth), jnp.float32)

    STAGE[...] = jnp.zeros(STAGE.shape, jnp.float32)

    pl.semaphore_wait(barrier, tiles - 1)

    above_tile = jnp.minimum(tile + 1, tiles - 1)
    below_tile = jnp.maximum(tile - 1, 0)
    above_id = (above_tile // members, lax.rem(above_tile, members))
    below_id = (below_tile // members, lax.rem(below_tile, members))

    def to_above(src, dst, index):
        return pltpu.make_async_remote_copy(
            src_ref=src,
            dst_ref=dst,
            send_sem=halo_send.at[index],
            recv_sem=halo_recv.at[index],
            device_id=above_id,
            device_id_type=MESH,
        )

    def to_below(src, dst, index):
        return pltpu.make_async_remote_copy(
            src_ref=src,
            dst_ref=dst,
            send_sem=halo_send.at[index],
            recv_sem=halo_recv.at[index],
            device_id=below_id,
            device_id_type=MESH,
        )

    def field_up(it, depth):
        return to_above(
            R.at[it, :, HALO + layers - 1 - depth],
            R.at[it, :, HALO - 1 - depth],
            2 + it * 4 + depth,
        )

    def field_down(it, depth):
        return to_below(
            R.at[it, :, HALO + depth], R.at[it, :, HALO + layers + depth], 4 + it * 4 + depth
        )

    phases_up = to_above(phases.at[layers - 3 : layers], PH.at[0:3], 0)
    phases_down = to_below(phases.at[0:2], PH.at[3:5], 1)

    def start_field(it):
        for depth in range(HALO):

            @pl.when(has_above)
            def _():
                field_up(it, depth).start()

            @pl.when(has_below)
            def _():
                field_down(it, depth).start()

    def wait_field(it, depth):
        @pl.when(has_above)
        def _():
            field_up(it, depth).wait_send()
            field_down(it, depth).wait_recv()

        @pl.when(has_below)
        def _():
            field_down(it, depth).wait_send()
            field_up(it, depth).wait_recv()

    @pl.when(has_above)
    def _():
        phases_up.start()

    @pl.when(has_below)
    def _():
        phases_down.start()

    start_field(0)

    lanes = coarse_height * coarse_breadth
    fine_at = lax.broadcasted_iota(jnp.int32, (breadth, lanes), 0)
    lane_at = lax.broadcasted_iota(jnp.int32, (breadth, lanes), 1)
    gather_x = jnp.where(
        fine_at // COARSEN == lax.rem(lane_at, coarse_breadth), 1.0, 0.0
    ).astype(jnp.float32)
    coarse_at = lax.broadcasted_iota(jnp.int32, (lanes, breadth), 0)
    column_at = lax.broadcasted_iota(jnp.int32, (lanes, breadth), 1)
    spread_x = jnp.where(
        lax.rem(coarse_at, coarse_breadth) == column_at // COARSEN, 1.0, 0.0
    ).astype(jnp.float32)
    row_mask = jnp.where(
        lax.broadcasted_iota(jnp.int32, (coarse_height, lanes), 0)
        == lax.broadcasted_iota(jnp.int32, (coarse_height, lanes), 1) // coarse_breadth,
        1.0,
        0.0,
    ).astype(jnp.float32)

    def block_row(plane):
        summed = jnp.sum(plane.reshape(coarse_height, COARSEN, breadth), axis=1)
        wide = jnp.dot(
            summed, gather_x, precision=lax.Precision.HIGHEST, preferred_element_type=jnp.float32
        )
        return jnp.sum(wide * row_mask, axis=0, keepdims=True)

    def block_plane(row):
        wide = jnp.broadcast_to(row, (coarse_height, lanes)) * row_mask
        narrow = jnp.dot(
            wide, spread_x, precision=lax.Precision.HIGHEST, preferred_element_type=jnp.float32
        )
        return jnp.broadcast_to(
            narrow[:, None, :], (coarse_height, COARSEN, breadth)
        ).reshape(height, breadth)

    lane_row = lax.broadcasted_iota(jnp.int32, (1, lanes), 1)
    coarse_keep = (
        (lane_row // coarse_breadth < coarse_height - 1)
        & (lax.rem(lane_row, coarse_breadth) < coarse_breadth - 1)
    )
    in_group = jnp.where(me < members - 1, 1.0 / (COARSEN**3), 0.0)
    coarse_row = jnp.where(coarse_keep, block_row(ACC[0]), 0.0) * in_group
    for it in range(2):
        STAGE[it, 3:4] = coarse_row

    @pl.when(has_above)
    def _():
        phases_up.wait_send()
        phases_down.wait_recv()

    @pl.when(has_below)
    def _():
        phases_down.wait_send()
        phases_up.wait_recv()

    for n in range(3):
        MOD[n] = moduli_of(PH[n], first_depth - 3 + n)
    for n in range(2):
        MOD[layers + 3 + n] = moduli_of(PH[3 + n], first_depth + layers + n)

    def back_x(value):
        return pltpu.roll(value, 1, 1)

    def back_y(value):
        return pltpu.roll(value, 1, 0)

    def fore_x(value):
        return pltpu.roll(value, breadth - 1, 1)

    def fore_y(value):
        return pltpu.roll(value, height - 1, 0)

    def free_at(n):
        return FREE[jnp.where(n == 0, 0, 1)]

    def inverse_layer(i, unused):
        pair = MOD[i] + MOD[i + 1]
        pair = pair + back_x(pair)
        pair = pair + back_y(pair)
        free = free_at(i - HALO)
        depth = first_depth + i - HALO
        valid = (depth >= 0) & (depth < tiles * layers)
        diagonal = jnp.where(valid, free * (entry * pair) + 1.0 - free, 1.0)
        W[i] = omega / diagonal
        return unused

    lax.fori_loop(0, layers + 2 * HALO, inverse_layer, 0)

    def modes_into(get, n):
        slot = lax.rem(n + 4, 2)
        free = free_at(n)
        for k in range(3):
            modes = plane_modes(free * get(k, n), fore_y, fore_x)
            for b in (0, 1):
                for c in (0, 1):
                    FWD[slot, 4 * k + 2 * b + c] = modes[b][c]

    def apply_stiffness(get, put, lowest, highest):
        modes_into(get, jnp.int32(lowest - 1))
        CARRY[...] = jnp.zeros(CARRY.shape, jnp.float32)

        def layer(v, unused):
            modes_into(get, v + 1)
            lower = lax.rem(v + 4, 2)
            upper = lax.rem(v + 5, 2)

            def chunk(j, nothing):
                rows = pl.ds(pl.multiple_of(j * 8, 8), 8)

                def of(slot):
                    return [
                        [[FWD[slot, 4 * k + 2 * b + c, rows] for c in (0, 1)] for b in (0, 1)]
                        for k in range(3)
                    ]

                low, high = voxel_forces(of(lower), of(upper), MOD[v + 3, rows], 1.0)
                for k in range(3):
                    for b in (0, 1):
                        for c in (0, 1):
                            index = 4 * k + 2 * b + c
                            FSUM[index, rows] = CARRY[index, rows] + low[k][b][c]
                            CARRY[index, rows] = high[k][b][c]
                return nothing

            lax.fori_loop(0, height // 8, chunk, 0, unroll=True)

            @pl.when(v >= lowest)
            def _():
                free = free_at(v)
                for k in range(3):
                    force = [[FSUM[4 * k + 2 * b + c] for c in (0, 1)] for b in (0, 1)]
                    total = plane_forces(force, back_y, back_x)
                    put(k, v, free * total + (1.0 - free) * get(k, v))

            return unused

        lax.fori_loop(lowest - 1, highest + 1, layer, 0)

    def coarse_ahead(value, by):
        return pltpu.roll(value, lanes - by, 2)

    def coarse_behind(value, by):
        return pltpu.roll(value, by, 2)

    def coarse_apply(field, mod):
        fore = (
            functools.partial(coarse_ahead, by=coarse_breadth),
            functools.partial(coarse_ahead, by=1),
        )
        back = (
            functools.partial(coarse_behind, by=coarse_breadth),
            functools.partial(coarse_behind, by=1),
        )
        below = [plane_modes(field[k], *fore) for k in range(3)]
        above = [
            [[pltpu.roll(below[k][b][c], members - 1, 1) for c in (0, 1)] for b in (0, 1)]
            for k in range(3)
        ]
        low, high = voxel_forces(below, above, mod, float(COARSEN))
        out = []
        for k in range(3):
            force = [
                [low[k][b][c] + pltpu.roll(high[k][b][c], 1, 1) for c in (0, 1)] for b in (0, 1)
            ]
            out.append(plane_forces(force, *back))
        return out

    def coarse_solve(it):
        mod = GAT[it, :, :, 3, :]
        rhs = [GAT[it, :, :, k, :] for k in range(3)]
        pair = mod + pltpu.roll(mod, 1, 1)
        pair = pair + coarse_behind(pair, 1)
        pair = pair + coarse_behind(pair, coarse_breadth)
        diagonal = (COARSEN * entry) * pair
        present = diagonal > 0.0
        inverse = jnp.where(present, 1.0 / jnp.where(present, diagonal, 1.0), 0.0)
        low_end = bound / 20.0
        center = 0.5 * (bound + low_end)
        radius = 0.5 * (bound - low_end)
        sigma = center / radius
        rho = 1.0 / sigma
        update = [inverse * rhs[k] * (1.0 / center) for k in range(3)]
        correction = update
        remainder = rhs
        for sweep in range(CHEB - 1):
            image = coarse_apply(update, mod)
            remainder = [remainder[k] - image[k] for k in range(3)]
            rho_next = 1.0 / (2.0 * sigma - rho)
            update = [
                (rho_next * rho) * update[k] + (2.0 * rho_next / radius) * (inverse * remainder[k])
                for k in range(3)
            ]
            correction = [correction[k] + update[k] for k in range(3)]
            rho = rho_next
        return correction

    def peer_copy(it, o, src):
        other = lax.rem(me + o, members)
        return pltpu.make_async_remote_copy(
            src_ref=src,
            dst_ref=GAT.at[it, 0, me],
            send_sem=gat_send.at[it, o],
            recv_sem=gat_recv.at[it, me],
            device_id=(grp, other),
            device_id_type=MESH,
        )

    def peer_arrival(it, sender):
        return pltpu.make_async_remote_copy(
            src_ref=STAGE.at[it],
            dst_ref=GAT.at[it, 0, sender],
            send_sem=gat_send.at[it, 0],
            recv_sem=gat_recv.at[it, sender],
            device_id=(grp, sender),
            device_id_type=MESH,
        )

    def cross_copy(it, side, sender, target):
        return pltpu.make_async_remote_copy(
            src_ref=STAGE.at[it],
            dst_ref=GAT.at[it, 1, sender],
            send_sem=cross_send.at[it, side],
            recv_sem=cross_recv.at[it, sender],
            device_id=target,
            device_id_type=MESH,
        )

    under = (jnp.maximum(grp - 1, 0), members - 1)
    over = (jnp.minimum(grp + 1, groups - 1), 0)

    def gather_rows(it):
        def send(o, unused):
            peer_copy(it, o, STAGE.at[it]).start()
            return unused

        lax.fori_loop(1, members, send, 0)

        @pl.when(grp > 0)
        def _():
            cross_copy(it, 0, me, under).start()

        @pl.when(grp < groups - 1)
        def _():
            cross_copy(it, 1, me, over).start()

        GAT[it, 0, me] = STAGE[it]

        def arrive(o, unused):
            peer_copy(it, o, STAGE.at[it]).wait_send()
            peer_arrival(it, lax.rem(me + o, members)).wait_recv()
            return unused

        lax.fori_loop(1, members, arrive, 0)

        @pl.when(grp > 0)
        def _():
            cross_copy(it, 0, me, under).wait_send()

        @pl.when(grp < groups - 1)
        def _():
            cross_copy(it, 1, me, over).wait_send()

        @pl.when(((me == members - 1) & (grp < groups - 1)) | ((me == 0) & (grp > 0)))
        def _():
            def arrive_cross(sender, unused):
                cross_copy(it, 0, sender, under).wait_recv()
                return unused

            lax.fori_loop(0, members, arrive_cross, 0)

    for it in range(2):
        if it == 1:
            start_field(1)
        wait_field(it, 0)

        for k in range(3):
            ACC[k] = jnp.zeros((height, breadth), jnp.float32)

        def first_of(k, n, it=it):
            return W[n + HALO] * R[it, k, n + HALO]

        def add_defect(k, n, value, it=it):
            ACC[k] = ACC[k] + (R[it, k, n + HALO] - value)

        apply_stiffness(first_of, add_defect, 0, layers - 1)
        for k in range(3):
            STAGE[it, k : k + 1] = block_row(ACC[k])
        gather_rows(it)
        correction = coarse_solve(it)
        member_at = lax.broadcasted_iota(jnp.int32, (members, lanes), 0)
        for k in range(3):
            own, other = correction[k][0], correction[k][1]

            def row_of(field, index):
                return jnp.sum(jnp.where(member_at == index, field, 0.0), axis=0, keepdims=True)

            under_row = jnp.where(me == 0, row_of(other, members - 1), row_of(own, me - 1))
            over_row = jnp.where(me == members - 1, row_of(other, 0), row_of(own, me + 1))
            PRO[0, k] = block_plane(under_row)
            PRO[1, k] = block_plane(row_of(own, me))
            PRO[2, k] = block_plane(over_row)

        wait_field(it, 1)

        def second_of(k, n, it=it):
            block = jnp.where(n < 0, 0, jnp.where(n >= layers, 2, 1))
            return first_of(k, n, it) + free_at(n) * PRO[block, k]

        def smooth(k, n, value, it=it):
            S[it, k, n + HALO] = second_of(k, n, it) + W[n + HALO] * (
                R[it, k, n + HALO] - value
            )

        apply_stiffness(second_of, smooth, -1, layers)

        def smoothed_of(k, n, it=it):
            return S[it, k, n + HALO]

        def keep_image(k, n, value, it=it):
            R[it + 1, k, n + HALO] = value

        apply_stiffness(smoothed_of, keep_image, 0, layers - 1)

    ACC[...] = jnp.zeros(ACC.shape, jnp.float32)

    def products(n, unused):
        i = n + HALO
        for k in range(3):
            r, q, t = R[0, k, i], R[1, k, i], R[2, k, i]
            p, s = S[0, k, i], S[1, k, i]
            for index, value in enumerate((r * p, p * q, r * s, q * s, p * t, s * t)):
                ACC[index] = ACC[index] + value
        return unused

    lax.fori_loop(0, layers, products, 0)
    DSUM[...] = jnp.zeros(DSUM.shape, jnp.float32)
    for index in range(6):
        DSUM[0, index : index + 1] = jnp.sum(ACC[index], axis=0, keepdims=True)

    def dot_copy(o):
        return pltpu.make_async_remote_copy(
            src_ref=DSUM.at[0],
            dst_ref=DOT.at[me],
            send_sem=dot_send.at[o],
            recv_sem=dot_recv.at[me],
            device_id=(grp, lax.rem(me + o, members)),
            device_id_type=MESH,
        )

    def dot_arrival(sender):
        return pltpu.make_async_remote_copy(
            src_ref=DSUM.at[0],
            dst_ref=DOT.at[sender],
            send_sem=dot_send.at[0],
            recv_sem=dot_recv.at[sender],
            device_id=(grp, sender),
            device_id_type=MESH,
        )

    def dotg_copy(o):
        return pltpu.make_async_remote_copy(
            src_ref=DSUM.at[1],
            dst_ref=DOTG.at[grp],
            send_sem=dotg_send.at[o],
            recv_sem=dotg_recv.at[grp],
            device_id=(lax.rem(grp + o, groups), me),
            device_id_type=MESH,
        )

    def dotg_arrival(sender):
        return pltpu.make_async_remote_copy(
            src_ref=DSUM.at[1],
            dst_ref=DOTG.at[sender],
            send_sem=dotg_send.at[0],
            recv_sem=dotg_recv.at[sender],
            device_id=(sender, me),
            device_id_type=MESH,
        )

    def exchange(copy, arrival, own, size):
        def send(o, unused):
            copy(o).start()
            return unused

        def arrive(o, unused):
            copy(o).wait_send()
            arrival(lax.rem(own + o, size)).wait_recv()
            return unused

        lax.fori_loop(1, size, send, 0)
        return lambda: lax.fori_loop(1, size, arrive, 0)

    finish = exchange(dot_copy, dot_arrival, me, members)
    DOT[me] = DSUM[0]
    finish()
    DSUM[1] = jnp.sum(DOT[...], axis=0)
    finish = exchange(dotg_copy, dotg_arrival, grp, groups)
    DOTG[grp] = DSUM[1]
    finish()
    sums = jnp.sum(jnp.sum(DOTG[...], axis=0), axis=1, keepdims=True)
    rp, pq, rs, qs, pt, st = [sums[index : index + 1] for index in range(6)]
    alpha = rp / pq
    following = rp - alpha * (rs + pq) + alpha * alpha * qs
    curve = pq - alpha * (pt + qs) + alpha * alpha * st
    beta = following / rp
    alpha_two = following / (curve - beta * following / alpha)
    weight_a = alpha + alpha_two * (1.0 + beta)
    weight_b = alpha * alpha_two

    def finish_layer(n, unused):
        i = n + HALO
        for k in range(3):
            out_u[k, n] = weight_a * S[0, k, i] - weight_b * S[1, k, i]
            out_r[k, n] = R[0, k, i] - weight_a * R[1, k, i] + weight_b * R[2, k, i]
        return unused

    lax.fori_loop(0, layers, finish_layer, 0)


def body(groups, members, load, phases, clamp, phase_moduli):
    _, layers, height, breadth = load.shape
    assert layers == COARSEN
    plane = (height, breadth)
    deep = layers + 2 * HALO
    lanes = (height // COARSEN) * (breadth // COARSEN)
    vmem = pl.BlockSpec(memory_space=pltpu.VMEM)
    dma = pltpu.SemaphoreType.DMA
    f32 = jnp.float32
    return tuple(
        pl.pallas_call(
            functools.partial(kernel, groups, members),
            out_shape=(
                jax.ShapeDtypeStruct(load.shape, f32),
                jax.ShapeDtypeStruct(load.shape, f32),
            ),
            in_specs=[vmem, vmem, vmem, pl.BlockSpec(memory_space=pltpu.SMEM)],
            out_specs=(vmem, vmem),
            scratch_shapes=[
                pltpu.VMEM((3, 3, deep) + plane, f32),
                pltpu.VMEM((2, 3, deep) + plane, f32),
                pltpu.VMEM((deep,) + plane, f32),
                pltpu.VMEM((deep + 1,) + plane, f32),
                pltpu.VMEM((5,) + plane, jnp.int32),
                pltpu.VMEM((2,) + plane, f32),
                pltpu.VMEM((3, 3) + plane, f32),
                pltpu.VMEM((2, 12) + plane, f32),
                pltpu.VMEM((12,) + plane, f32),
                pltpu.VMEM((12,) + plane, f32),
                pltpu.VMEM((6,) + plane, f32),
                pltpu.VMEM((2, 8, lanes), f32),
                pltpu.VMEM((2, 2, members, 8, lanes), f32),
                pltpu.VMEM((members, 8, breadth), f32),
                pltpu.VMEM((2, 8, breadth), f32),
                pltpu.VMEM((groups, 8, breadth), f32),
                dma((10,)),
                dma((10,)),
                dma((2, members)),
                dma((2, members)),
                dma((2, 2)),
                dma((2, members)),
                dma((members,)),
                dma((members,)),
                dma((groups,)),
                dma((groups,)),
            ],
            compiler_params=pltpu.CompilerParams(
                collective_id=0, has_side_effects=True, vmem_limit_bytes=48 * 1024 * 1024
            ),
        )(load, phases, clamp, phase_moduli)
    )


def solution(mesh):
    groups, members = mesh.shape["grp"], mesh.shape["gz"]
    placed = (P(None, ("grp", "gz"), None, None), P(("grp", "gz"), None, None), P(), P())
    return jax.shard_map(
        functools.partial(body, groups, members),
        mesh=mesh,
        in_specs=placed,
        out_specs=(P(None, ("grp", "gz"), None, None), P(None, ("grp", "gz"), None, None)),
        check_vma=False,
    )
```

```python
import functools
import math

import jax
import jax.numpy as jnp
import numpy as np
from jax import lax
from jax.experimental import pallas as pl
from jax.experimental.pallas import tpu as pltpu
from jax.sharding import PartitionSpec as P

PHASES = 4
COARSEN = 8
CHEB = 4
ITERS = 2
HALO = 2
MESH = pl.DeviceIdType.MESH

POISSON = 0.3
LAME = POISSON / ((1.0 + POISSON) * (1.0 - 2.0 * POISSON))
SHEAR = 1.0 / (2.0 * (1.0 + POISSON))


CORNER_OFFSETS = [
    (along_z, along_y, along_x) for along_z in (0, 1) for along_y in (0, 1) for along_x in (0, 1)
]


def element_matrix():
    elastic = np.zeros((6, 6))
    elastic[:3, :3] = LAME
    for axis_one in range(3):
        elastic[axis_one, axis_one] = LAME + 2.0 * SHEAR
        elastic[axis_one + 3, axis_one + 3] = SHEAR
    points = [0.5 - 0.5 / math.sqrt(3.0), 0.5 + 0.5 / math.sqrt(3.0)]
    pairs = [(0, 1), (1, 2), (0, 2)]
    matrix = np.zeros((24, 24))
    for first_point in points:
        for second_point in points:
            for third_point in points:
                spot = (first_point, second_point, third_point)
                strain = np.zeros((6, 24))
                for corner, offset in enumerate(CORNER_OFFSETS):
                    values = [
                        spot[axis_one] if offset[axis_one] else 1.0 - spot[axis_one]
                        for axis_one in range(3)
                    ]
                    slopes = [1.0 if offset[axis_one] else -1.0 for axis_one in range(3)]
                    slants = []
                    for axis_one in range(3):
                        others = [values[axis_two] for axis_two in range(3) if axis_two != axis_one]
                        slants.append(slopes[axis_one] * others[0] * others[1])
                        strain[axis_one, 3 * corner + axis_one] = slants[axis_one]
                    for position, pair in enumerate(pairs):
                        strain[3 + position, 3 * corner + pair[0]] = slants[pair[1]]
                        strain[3 + position, 3 * corner + pair[1]] = slants[pair[0]]
                matrix = matrix + 0.125 * (strain.T @ elastic @ strain)
    return matrix


def spectral_bound(numbers):
    diagonal_part = np.array([numbers[index, index] for index in range(numbers.shape[0])])
    return float(np.max(np.sum(np.abs(numbers), axis=1) / diagonal_part))


def voxel_forces(below, above, mod, scale):
    one, two, three = scale / 16.0, scale / 48.0, scale / 144.0
    u = []
    for k in range(3):
        modes = {}
        for b in (0, 1):
            for c in (0, 1):
                if b or c:
                    modes[(0, b, c)] = below[k][b][c] + above[k][b][c]
                modes[(1, b, c)] = above[k][b][c] - below[k][b][c]
        u.append(modes)
    unit = [(1, 0, 0), (0, 1, 0), (0, 0, 1)]

    def pair(i, j):
        return tuple(unit[i][d] + unit[j][d] for d in range(3))

    f = [{}, {}, {}]
    trace = (mod * (one * LAME)) * (u[0][unit[0]] + u[1][unit[1]] + u[2][unit[2]])
    stretch = mod * (2.0 * one * SHEAR)
    slide = mod * (one * SHEAR)
    for k in range(3):
        f[k][unit[k]] = trace + stretch * u[k][unit[k]]
    for i, j in ((0, 1), (1, 2), (0, 2)):
        shear = slide * (u[i][unit[j]] + u[j][unit[i]])
        f[i][unit[j]] = shear
        f[j][unit[i]] = shear
    same = mod * (two * (LAME + 3.0 * SHEAR))
    cross = mod * (two * LAME)
    for k in range(3):
        for m in range(3):
            if m != k:
                j = 3 - k - m
                f[k][pair(k, m)] = same * u[k][pair(k, m)] + cross * u[j][pair(j, m)]
    twist = mod * (two * SHEAR)
    total = u[0][pair(1, 2)] + u[1][pair(0, 2)] + u[2][pair(0, 1)]
    for k in range(3):
        i, j = [d for d in range(3) if d != k]
        f[k][pair(i, j)] = twist * (u[k][pair(i, j)] + total)
    warp = mod * (three * (LAME + 4.0 * SHEAR))
    for k in range(3):
        f[k][(1, 1, 1)] = warp * u[k][(1, 1, 1)]
    low = [[[None, None], [None, None]] for k in range(3)]
    high = [[[None, None], [None, None]] for k in range(3)]
    for k in range(3):
        for b in (0, 1):
            for c in (0, 1):
                if b or c:
                    low[k][b][c] = f[k][(0, b, c)] - f[k][(1, b, c)]
                    high[k][b][c] = f[k][(0, b, c)] + f[k][(1, b, c)]
                else:
                    low[k][b][c] = -f[k][(1, b, c)]
                    high[k][b][c] = f[k][(1, b, c)]
    return low, high


def plane_modes(value, ahead_y, ahead_x):
    shifted = ahead_x(value)
    rows = [value + shifted, shifted - value]
    out = [[None, None], [None, None]]
    for c in (0, 1):
        up = ahead_y(rows[c])
        out[0][c] = rows[c] + up
        out[1][c] = up - rows[c]
    return out


def plane_forces(force, behind_y, behind_x):
    rows = [
        (force[0][c] - force[1][c]) + behind_y(force[0][c] + force[1][c]) for c in (0, 1)
    ]
    return (rows[0] - rows[1]) + behind_x(rows[0] + rows[1])


def kernel(
    groups,
    members,
    load,
    phases,
    clamp,
    phase_moduli,
    out_u,
    out_r,
    R,
    LABEL,
    HELD,
    PART,
    SEAM,
    S,
    W,
    MOD,
    PH,
    FREE,
    PRO,
    ACC,
    STAGE,
    GAT,
    DOT,
    DSUM,
    DOTG,
    in_sem,
    halo_send,
    halo_recv,
    gat_send,
    gat_recv,
    cross_send,
    cross_recv,
    dot_send,
    dot_recv,
    dotg_send,
    dotg_recv,
):
    numbers = element_matrix()
    entry = float(numbers[0, 0])
    bound = spectral_bound(numbers)
    omega = 1.2 / bound
    _, layers, height, breadth = load.shape
    coarse_height = height // COARSEN
    coarse_breadth = breadth // COARSEN
    grp = lax.axis_index("grp")
    me = lax.axis_index("gz")
    tile = grp * members + me
    tiles = groups * members
    has_below = tile > 0
    has_above = tile < tiles - 1

    GAT[...] = jnp.zeros(GAT.shape, jnp.float32)
    barrier = pltpu.get_barrier_semaphore()

    def greet(o, unused):
        other = lax.rem(tile + o, tiles)
        pl.semaphore_signal(
            barrier,
            inc=1,
            device_id=(other // members, lax.rem(other, members)),
            device_id_type=MESH,
        )
        return unused

    lax.fori_loop(1, tiles, greet, 0)

    incoming = [
        pltpu.make_async_copy(load, R.at[0, :, HALO : HALO + layers], in_sem.at[0]),
        pltpu.make_async_copy(phases, LABEL, in_sem.at[1]),
        pltpu.make_async_copy(clamp, HELD, in_sem.at[2]),
    ]
    for copy in incoming:
        copy.start()

    @pl.when(tile == 0)
    def _():
        PH[0:3] = jnp.zeros((3, height, breadth), jnp.int32)
        for it in range(2):
            R[it, :, 0:HALO] = jnp.zeros((3, HALO, height, breadth), jnp.float32)

    @pl.when(tile == tiles - 1)
    def _():
        PH[3:5] = jnp.zeros((2, height, breadth), jnp.int32)
        for it in range(2):
            R[it, :, layers + HALO :] = jnp.zeros((3, HALO, height, breadth), jnp.float32)

    STAGE[...] = jnp.zeros(STAGE.shape, jnp.float32)
    for copy in incoming:
        copy.wait()
    first_depth = tile * layers
    bottom = jnp.where(tile == 0, 1.0, 0.0)
    free_plane = 1.0 - jnp.where(HELD[...] == 1, 1.0, 0.0) * bottom
    FREE[...] = free_plane
    for k in range(3):
        R[0, k, HALO] = free_plane * R[0, k, HALO]

    pl.semaphore_wait(barrier, tiles - 1)

    above_tile = jnp.minimum(tile + 1, tiles - 1)
    below_tile = jnp.maximum(tile - 1, 0)
    above_id = (above_tile // members, lax.rem(above_tile, members))
    below_id = (below_tile // members, lax.rem(below_tile, members))

    def to_above(src, dst, index):
        return pltpu.make_async_remote_copy(
            src_ref=src,
            dst_ref=dst,
            send_sem=halo_send.at[index],
            recv_sem=halo_recv.at[index],
            device_id=above_id,
            device_id_type=MESH,
        )

    def to_below(src, dst, index):
        return pltpu.make_async_remote_copy(
            src_ref=src,
            dst_ref=dst,
            send_sem=halo_send.at[index],
            recv_sem=halo_recv.at[index],
            device_id=below_id,
            device_id_type=MESH,
        )

    def field_up(it, depth):
        return to_above(
            R.at[it, :, HALO + layers - 1 - depth],
            R.at[it, :, HALO - 1 - depth],
            2 + it * 4 + depth,
        )

    def field_down(it, depth):
        return to_below(
            R.at[it, :, HALO + depth], R.at[it, :, HALO + layers + depth], 4 + it * 4 + depth
        )

    phases_up = to_above(LABEL.at[layers - 3 : layers], PH.at[0:3], 0)
    phases_down = to_below(LABEL.at[0:2], PH.at[3:5], 1)

    def start_field(it):
        for depth in range(HALO):

            @pl.when(has_above)
            def _():
                field_up(it, depth).start()

            @pl.when(has_below)
            def _():
                field_down(it, depth).start()

    def wait_field(it, depth):
        @pl.when(has_above)
        def _():
            field_up(it, depth).wait_send()
            field_down(it, depth).wait_recv()

        @pl.when(has_below)
        def _():
            field_down(it, depth).wait_send()
            field_up(it, depth).wait_recv()

    @pl.when(has_above)
    def _():
        phases_up.start()

    @pl.when(has_below)
    def _():
        phases_down.start()

    start_field(0)

    rows_at = lax.broadcasted_iota(jnp.int32, (height, breadth), 0)
    columns_at = lax.broadcasted_iota(jnp.int32, (height, breadth), 1)
    inside = (rows_at < height - 1) & (columns_at < breadth - 1)

    def moduli_of(labels, depth):
        picked = jnp.zeros((height, breadth), jnp.float32)
        for phase in range(PHASES):
            picked = jnp.where(labels == phase, phase_moduli[phase], picked)
        keep = jnp.where((depth >= 0) & (depth < tiles * layers - 1), 1.0, 0.0)
        return jnp.where(inside, picked, 0.0) * keep

    ACC[0] = jnp.zeros((height, breadth), jnp.float32)

    def own_layer(n, unused):
        mod = moduli_of(LABEL[n], first_depth + n)
        MOD[n + 3] = mod
        ACC[0] = ACC[0] + mod
        return unused

    lax.fori_loop(0, layers, own_layer, 0)

    lanes = coarse_height * coarse_breadth
    fine_at = lax.broadcasted_iota(jnp.int32, (breadth, lanes), 0)
    lane_at = lax.broadcasted_iota(jnp.int32, (breadth, lanes), 1)
    gather_x = jnp.where(
        fine_at // COARSEN == lax.rem(lane_at, coarse_breadth), 1.0, 0.0
    ).astype(jnp.float32)
    coarse_at = lax.broadcasted_iota(jnp.int32, (lanes, breadth), 0)
    column_at = lax.broadcasted_iota(jnp.int32, (lanes, breadth), 1)
    spread_x = jnp.where(
        lax.rem(coarse_at, coarse_breadth) == column_at // COARSEN, 1.0, 0.0
    ).astype(jnp.float32)
    row_mask = jnp.where(
        lax.broadcasted_iota(jnp.int32, (coarse_height, lanes), 0)
        == lax.broadcasted_iota(jnp.int32, (coarse_height, lanes), 1) // coarse_breadth,
        1.0,
        0.0,
    ).astype(jnp.float32)

    def block_row(plane):
        summed = jnp.sum(plane.reshape(coarse_height, COARSEN, breadth), axis=1)
        wide = jnp.dot(
            summed, gather_x, precision=lax.Precision.HIGHEST, preferred_element_type=jnp.float32
        )
        return jnp.sum(wide * row_mask, axis=0, keepdims=True)

    def block_plane(row):
        wide = jnp.broadcast_to(row, (coarse_height, lanes)) * row_mask
        narrow = jnp.dot(
            wide, spread_x, precision=lax.Precision.HIGHEST, preferred_element_type=jnp.float32
        )
        return jnp.broadcast_to(
            narrow[:, None, :], (coarse_height, COARSEN, breadth)
        ).reshape(height, breadth)

    lane_row = lax.broadcasted_iota(jnp.int32, (1, lanes), 1)
    coarse_keep = (
        (lane_row // coarse_breadth < coarse_height - 1)
        & (lax.rem(lane_row, coarse_breadth) < coarse_breadth - 1)
    )
    in_group = jnp.where(me < members - 1, 1.0 / (COARSEN**3), 0.0)
    coarse_row = jnp.where(coarse_keep, block_row(ACC[0]), 0.0) * in_group
    for it in range(2):
        STAGE[it, 3:4] = coarse_row

    def back_x(value):
        return pltpu.roll(value, 1, 1)

    def back_y(value):
        return pltpu.roll(value, 1, 0)

    def fore_x(value):
        return pltpu.roll(value, breadth - 1, 1)

    def inverse_layer(n, free):
        pair = MOD[n + 2] + MOD[n + 3]
        pair = pair + back_x(pair)
        pair = pair + back_y(pair)
        depth = first_depth + n
        valid = (depth >= 0) & (depth < tiles * layers)
        diagonal = entry * pair
        if free is not None:
            diagonal = free * diagonal + 1.0 - free
        W[n + HALO] = omega / jnp.where(valid, diagonal, 1.0)

    def inverse_inner(n, unused):
        inverse_layer(n, None)
        return unused

    lax.fori_loop(1, layers, inverse_inner, 0)

    def halo_moduli():
        @pl.when(has_above)
        def _():
            phases_up.wait_send()
            phases_down.wait_recv()

        @pl.when(has_below)
        def _():
            phases_down.wait_send()
            phases_up.wait_recv()

        for n in range(3):
            MOD[n] = moduli_of(PH[n], first_depth - 3 + n)
        for n in range(2):
            MOD[layers + 3 + n] = moduli_of(PH[3 + n], first_depth + layers + n)
        for n in (-2, -1, 0, layers, layers + 1):
            inverse_layer(n, FREE[...] if n == 0 else None)

    chunks = height // 8
    row_at = lax.broadcasted_iota(jnp.int32, (8, breadth), 0)
    first_row = row_at == 0

    def sweep(get, put, start, stop, put_first=None, put_last=None):
        for n in range(start, stop + 1):
            for k in range(3):
                SEAM[n + HALO, k] = jnp.zeros((8, breadth), jnp.float32)

        def chunk(j, unused):
            rows = pl.ds(pl.multiple_of(j * 8, 8), 8)
            following_rows = pl.ds(pl.multiple_of(lax.rem(j + 1, chunks) * 8, 8), 8)

            def modes(n, masked):
                out = []
                for k in range(3):
                    here, after = get(k, n, rows), get(k, n, following_rows)
                    if masked:
                        here, after = FREE[rows] * here, FREE[following_rows] * after
                    over = pltpu.roll(jnp.where(first_row, after, here), 7, 0)
                    here_x, over_x = fore_x(here), fore_x(over)
                    sums = here + here_x, over + over_x
                    steps = here_x - here, over_x - over
                    out.append(
                        [
                            [sums[0] + sums[1], steps[0] + steps[1]],
                            [sums[1] - sums[0], steps[1] - steps[0]],
                        ]
                    )
                return out

            def emit(n, force, masked, to):
                for k in range(3):
                    e = [
                        (force[k][b][0] - force[k][b][1])
                        + back_x(force[k][b][0] + force[k][b][1])
                        for b in (0, 1)
                    ]
                    turned = pltpu.roll(e[0] + e[1], 1, 0)
                    total = (e[0] - e[1]) + jnp.where(first_row, SEAM[n + HALO, k], turned)
                    SEAM[n + HALO, k] = turned
                    if masked:
                        free = FREE[rows]
                        total = free * total + (1.0 - free) * get(k, n, rows)
                    to(k, n, rows, total)

            def step(v, below, carry, static):
                above = modes(v + 1, static and v + 1 == 0)
                low, high = voxel_forces(below, above, MOD[v + 3, rows], 1.0)
                if carry is None:
                    if put_first is not None:
                        emit(v, low, static and v == 0, put_first)
                else:
                    force = [
                        [[carry[k][b][c] + low[k][b][c] for c in (0, 1)] for b in (0, 1)]
                        for k in range(3)
                    ]
                    emit(v, force, static and v == 0, put)
                return above, high

            below, carry = modes(start, start == 0), None
            v = start
            while v < stop and (v <= max(start, 0)):
                below, carry = step(v, below, carry, True)
                v += 1
            if v < stop:

                def inner(at, state):
                    return step(at, state[0], state[1], False)

                below, carry = lax.fori_loop(v, stop, inner, (below, carry), unroll=True)
            if put_last is not None:
                emit(stop, carry, stop == 0, put_last)
            return unused

        lax.fori_loop(0, chunks, chunk, 0)

    def coarse_ahead(value, by):
        return pltpu.roll(value, lanes - by, 2)

    def coarse_behind(value, by):
        return pltpu.roll(value, by, 2)

    def coarse_apply(field, mod):
        fore = (
            functools.partial(coarse_ahead, by=coarse_breadth),
            functools.partial(coarse_ahead, by=1),
        )
        back = (
            functools.partial(coarse_behind, by=coarse_breadth),
            functools.partial(coarse_behind, by=1),
        )
        below = [plane_modes(field[k], *fore) for k in range(3)]
        above = [
            [[pltpu.roll(below[k][b][c], members - 1, 1) for c in (0, 1)] for b in (0, 1)]
            for k in range(3)
        ]
        low, high = voxel_forces(below, above, mod, float(COARSEN))
        out = []
        for k in range(3):
            force = [
                [low[k][b][c] + pltpu.roll(high[k][b][c], 1, 1) for c in (0, 1)] for b in (0, 1)
            ]
            out.append(plane_forces(force, *back))
        return out

    def coarse_solve(it):
        mod = GAT[it, :, :, 3, :]
        rhs = [GAT[it, :, :, k, :] for k in range(3)]
        pair = mod + pltpu.roll(mod, 1, 1)
        pair = pair + coarse_behind(pair, 1)
        pair = pair + coarse_behind(pair, coarse_breadth)
        diagonal = (COARSEN * entry) * pair
        present = diagonal > 0.0
        inverse = jnp.where(present, 1.0 / jnp.where(present, diagonal, 1.0), 0.0)
        low_end = bound / 20.0
        center = 0.5 * (bound + low_end)
        radius = 0.5 * (bound - low_end)
        sigma = center / radius
        rho = 1.0 / sigma
        update = [inverse * rhs[k] * (1.0 / center) for k in range(3)]
        correction = update
        remainder = rhs
        for sweep in range(CHEB - 1):
            image = coarse_apply(update, mod)
            remainder = [remainder[k] - image[k] for k in range(3)]
            rho_next = 1.0 / (2.0 * sigma - rho)
            update = [
                (rho_next * rho) * update[k] + (2.0 * rho_next / radius) * (inverse * remainder[k])
                for k in range(3)
            ]
            correction = [correction[k] + update[k] for k in range(3)]
            rho = rho_next
        return correction

    def peer_copy(it, o, src):
        other = lax.rem(me + o, members)
        return pltpu.make_async_remote_copy(
            src_ref=src,
            dst_ref=GAT.at[it, 0, me],
            send_sem=gat_send.at[it, o],
            recv_sem=gat_recv.at[it, me],
            device_id=(grp, other),
            device_id_type=MESH,
        )

    def peer_arrival(it, sender):
        return pltpu.make_async_remote_copy(
            src_ref=STAGE.at[it],
            dst_ref=GAT.at[it, 0, sender],
            send_sem=gat_send.at[it, 0],
            recv_sem=gat_recv.at[it, sender],
            device_id=(grp, sender),
            device_id_type=MESH,
        )

    def cross_copy(it, side, sender, target):
        return pltpu.make_async_remote_copy(
            src_ref=STAGE.at[it],
            dst_ref=GAT.at[it, 1, sender],
            send_sem=cross_send.at[it, side],
            recv_sem=cross_recv.at[it, sender],
            device_id=target,
            device_id_type=MESH,
        )

    under = (jnp.maximum(grp - 1, 0), members - 1)
    over = (jnp.minimum(grp + 1, groups - 1), 0)

    def gather_rows(it):
        def send(o, unused):
            peer_copy(it, o, STAGE.at[it]).start()
            return unused

        lax.fori_loop(1, members, send, 0)

        @pl.when(grp > 0)
        def _():
            cross_copy(it, 0, me, under).start()

        @pl.when(grp < groups - 1)
        def _():
            cross_copy(it, 1, me, over).start()

        GAT[it, 0, me] = STAGE[it]

        def arrive(o, unused):
            peer_copy(it, o, STAGE.at[it]).wait_send()
            peer_arrival(it, lax.rem(me + o, members)).wait_recv()
            return unused

        lax.fori_loop(1, members, arrive, 0)

        @pl.when(grp > 0)
        def _():
            cross_copy(it, 0, me, under).wait_send()

        @pl.when(grp < groups - 1)
        def _():
            cross_copy(it, 1, me, over).wait_send()

        @pl.when(((me == members - 1) & (grp < groups - 1)) | ((me == 0) & (grp > 0)))
        def _():
            def arrive_cross(sender, unused):
                cross_copy(it, 0, sender, under).wait_recv()
                return unused

            lax.fori_loop(0, members, arrive_cross, 0)

    for it in range(2):
        if it == 1:
            start_field(1)

        for k in range(3):
            ACC[k] = jnp.zeros((height, breadth), jnp.float32)

        def first_of(k, n, rows, it=it):
            return W[n + HALO, rows] * R[it, k, n + HALO, rows]

        def add_defect(k, n, rows, value, it=it):
            ACC[k, rows] = ACC[k, rows] + (R[it, k, n + HALO, rows] - value)

        def part(index):
            def to(k, n, rows, value):
                PART[index, k, rows] = value

            return to

        def with_part(index):
            def to(k, n, rows, value):
                add_defect(k, n, rows, PART[index, k, rows] + value)

            return to

        sweep(first_of, add_defect, 1, layers - 1, part(0), part(1))
        if it == 0:
            halo_moduli()
        wait_field(it, 0)
        sweep(first_of, add_defect, -1, 1, None, with_part(0))
        sweep(first_of, add_defect, layers - 1, layers, with_part(1), None)
        for k in range(3):
            STAGE[it, k : k + 1] = block_row(ACC[k])
        gather_rows(it)
        correction = coarse_solve(it)
        member_at = lax.broadcasted_iota(jnp.int32, (members, lanes), 0)
        for k in range(3):
            own, other = correction[k][0], correction[k][1]

            def row_of(field, index):
                return jnp.sum(jnp.where(member_at == index, field, 0.0), axis=0, keepdims=True)

            under_row = jnp.where(me == 0, row_of(other, members - 1), row_of(own, me - 1))
            over_row = jnp.where(me == members - 1, row_of(other, 0), row_of(own, me + 1))
            PRO[0, k] = block_plane(under_row)
            PRO[1, k] = block_plane(row_of(own, me))
            PRO[2, k] = block_plane(over_row)

        wait_field(it, 1)

        def second_of(k, n, rows, it=it):
            block = jnp.where(n < 0, 0, jnp.where(n >= layers, 2, 1))
            spread = PRO[block, k, rows]
            if isinstance(n, int) and n == 0:
                spread = FREE[rows] * spread
            return first_of(k, n, rows, it) + spread

        def smooth(k, n, rows, value, it=it):
            S[it, k, n + HALO, rows] = second_of(k, n, rows, it) + W[n + HALO, rows] * (
                R[it, k, n + HALO, rows] - value
            )

        sweep(second_of, smooth, -2, layers + 1)

        def smoothed_of(k, n, rows, it=it):
            return S[it, k, n + HALO, rows]

        def keep_image(k, n, rows, value, it=it):
            R[it + 1, k, n + HALO, rows] = value

        sweep(smoothed_of, keep_image, -1, layers)

    ACC[...] = jnp.zeros(ACC.shape, jnp.float32)

    def products(n, unused):
        i = n + HALO
        for k in range(3):
            r, q, t = R[0, k, i], R[1, k, i], R[2, k, i]
            p, s = S[0, k, i], S[1, k, i]
            for index, value in enumerate((r * p, p * q, r * s, q * s, p * t, s * t)):
                ACC[index] = ACC[index] + value
        return unused

    lax.fori_loop(0, layers, products, 0)
    DSUM[...] = jnp.zeros(DSUM.shape, jnp.float32)
    for index in range(6):
        DSUM[0, index : index + 1] = jnp.sum(ACC[index], axis=0, keepdims=True)

    def dot_copy(o):
        return pltpu.make_async_remote_copy(
            src_ref=DSUM.at[0],
            dst_ref=DOT.at[me],
            send_sem=dot_send.at[o],
            recv_sem=dot_recv.at[me],
            device_id=(grp, lax.rem(me + o, members)),
            device_id_type=MESH,
        )

    def dot_arrival(sender):
        return pltpu.make_async_remote_copy(
            src_ref=DSUM.at[0],
            dst_ref=DOT.at[sender],
            send_sem=dot_send.at[0],
            recv_sem=dot_recv.at[sender],
            device_id=(grp, sender),
            device_id_type=MESH,
        )

    def dotg_copy(o):
        return pltpu.make_async_remote_copy(
            src_ref=DSUM.at[1],
            dst_ref=DOTG.at[grp],
            send_sem=dotg_send.at[o],
            recv_sem=dotg_recv.at[grp],
            device_id=(lax.rem(grp + o, groups), me),
            device_id_type=MESH,
        )

    def dotg_arrival(sender):
        return pltpu.make_async_remote_copy(
            src_ref=DSUM.at[1],
            dst_ref=DOTG.at[sender],
            send_sem=dotg_send.at[0],
            recv_sem=dotg_recv.at[sender],
            device_id=(sender, me),
            device_id_type=MESH,
        )

    def exchange(copy, arrival, own, size):
        def send(o, unused):
            copy(o).start()
            return unused

        def arrive(o, unused):
            copy(o).wait_send()
            arrival(lax.rem(own + o, size)).wait_recv()
            return unused

        lax.fori_loop(1, size, send, 0)
        return lambda: lax.fori_loop(1, size, arrive, 0)

    finish = exchange(dot_copy, dot_arrival, me, members)
    DOT[me] = DSUM[0]
    finish()
    DSUM[1] = jnp.sum(DOT[...], axis=0)
    finish = exchange(dotg_copy, dotg_arrival, grp, groups)
    DOTG[grp] = DSUM[1]
    finish()
    sums = jnp.sum(jnp.sum(DOTG[...], axis=0), axis=1, keepdims=True)
    rp, pq, rs, qs, pt, st = [sums[index : index + 1] for index in range(6)]
    alpha = rp / pq
    following = rp - alpha * (rs + pq) + alpha * alpha * qs
    curve = pq - alpha * (pt + qs) + alpha * alpha * st
    beta = following / rp
    alpha_two = following / (curve - beta * following / alpha)
    weight_a = alpha + alpha_two * (1.0 + beta)
    weight_b = alpha * alpha_two

    def finish_layer(n, unused):
        i = n + HALO
        for k in range(3):
            out_u[k, n] = weight_a * S[0, k, i] - weight_b * S[1, k, i]
            out_r[k, n] = R[0, k, i] - weight_a * R[1, k, i] + weight_b * R[2, k, i]
        return unused

    lax.fori_loop(0, layers, finish_layer, 0)


def body(groups, members, load, phases, clamp, phase_moduli):
    _, layers, height, breadth = load.shape
    assert layers == COARSEN
    plane = (height, breadth)
    deep = layers + 2 * HALO
    lanes = (height // COARSEN) * (breadth // COARSEN)
    vmem = pl.BlockSpec(memory_space=pltpu.VMEM)
    hbm = pl.BlockSpec(memory_space=pltpu.HBM)
    dma = pltpu.SemaphoreType.DMA
    f32 = jnp.float32
    return tuple(
        pl.pallas_call(
            functools.partial(kernel, groups, members),
            out_shape=(
                jax.ShapeDtypeStruct(load.shape, f32),
                jax.ShapeDtypeStruct(load.shape, f32),
            ),
            in_specs=[hbm, hbm, hbm, pl.BlockSpec(memory_space=pltpu.SMEM)],
            out_specs=(vmem, vmem),
            scratch_shapes=[
                pltpu.VMEM((3, 3, deep) + plane, f32),
                pltpu.VMEM((layers,) + plane, jnp.int32),
                pltpu.VMEM(plane, jnp.int32),
                pltpu.VMEM((2, 3) + plane, f32),
                pltpu.VMEM((deep, 3, 8, breadth), f32),
                pltpu.VMEM((2, 3, deep) + plane, f32),
                pltpu.VMEM((deep,) + plane, f32),
                pltpu.VMEM((deep + 1,) + plane, f32),
                pltpu.VMEM((5,) + plane, jnp.int32),
                pltpu.VMEM(plane, f32),
                pltpu.VMEM((3, 3) + plane, f32),
                pltpu.VMEM((6,) + plane, f32),
                pltpu.VMEM((2, 8, lanes), f32),
                pltpu.VMEM((2, 2, members, 8, lanes), f32),
                pltpu.VMEM((members, 8, breadth), f32),
                pltpu.VMEM((2, 8, breadth), f32),
                pltpu.VMEM((groups, 8, breadth), f32),
                dma((3,)),
                dma((10,)),
                dma((10,)),
                dma((2, members)),
                dma((2, members)),
                dma((2, 2)),
                dma((2, members)),
                dma((members,)),
                dma((members,)),
                dma((groups,)),
                dma((groups,)),
            ],
            compiler_params=pltpu.CompilerParams(
                collective_id=0, has_side_effects=True, vmem_limit_bytes=48 * 1024 * 1024
            ),
        )(load, phases, clamp, phase_moduli)
    )


def solution(mesh):
    groups, members = mesh.shape["grp"], mesh.shape["gz"]
    placed = (P(None, ("grp", "gz"), None, None), P(("grp", "gz"), None, None), P(), P())
    return jax.shard_map(
        functools.partial(body, groups, members),
        mesh=mesh,
        in_specs=placed,
        out_specs=(P(None, ("grp", "gz"), None, None), P(None, ("grp", "gz"), None, None)),
        check_vma=False,
    )
```

```python
import functools
import math

import jax
import jax.numpy as jnp
import numpy as np
from jax import lax
from jax.experimental import pallas as pl
from jax.experimental.pallas import tpu as pltpu
from jax.sharding import PartitionSpec as P

PHASES = 4
COARSEN = 8
CHEB = 4
ITERS = 2
HALO = 2
MESH = pl.DeviceIdType.MESH

POISSON = 0.3
LAME = POISSON / ((1.0 + POISSON) * (1.0 - 2.0 * POISSON))
SHEAR = 1.0 / (2.0 * (1.0 + POISSON))


CORNER_OFFSETS = [
    (along_z, along_y, along_x) for along_z in (0, 1) for along_y in (0, 1) for along_x in (0, 1)
]


def element_matrix():
    elastic = np.zeros((6, 6))
    elastic[:3, :3] = LAME
    for axis_one in range(3):
        elastic[axis_one, axis_one] = LAME + 2.0 * SHEAR
        elastic[axis_one + 3, axis_one + 3] = SHEAR
    points = [0.5 - 0.5 / math.sqrt(3.0), 0.5 + 0.5 / math.sqrt(3.0)]
    pairs = [(0, 1), (1, 2), (0, 2)]
    matrix = np.zeros((24, 24))
    for first_point in points:
        for second_point in points:
            for third_point in points:
                spot = (first_point, second_point, third_point)
                strain = np.zeros((6, 24))
                for corner, offset in enumerate(CORNER_OFFSETS):
                    values = [
                        spot[axis_one] if offset[axis_one] else 1.0 - spot[axis_one]
                        for axis_one in range(3)
                    ]
                    slopes = [1.0 if offset[axis_one] else -1.0 for axis_one in range(3)]
                    slants = []
                    for axis_one in range(3):
                        others = [values[axis_two] for axis_two in range(3) if axis_two != axis_one]
                        slants.append(slopes[axis_one] * others[0] * others[1])
                        strain[axis_one, 3 * corner + axis_one] = slants[axis_one]
                    for position, pair in enumerate(pairs):
                        strain[3 + position, 3 * corner + pair[0]] = slants[pair[1]]
                        strain[3 + position, 3 * corner + pair[1]] = slants[pair[0]]
                matrix = matrix + 0.125 * (strain.T @ elastic @ strain)
    return matrix


def spectral_bound(numbers):
    diagonal_part = np.array([numbers[index, index] for index in range(numbers.shape[0])])
    return float(np.max(np.sum(np.abs(numbers), axis=1) / diagonal_part))


def voxel_forces(below, above, mod, scale):
    one, two, three = scale / 16.0, scale / 48.0, scale / 144.0
    u = []
    for k in range(3):
        modes = {}
        for b in (0, 1):
            for c in (0, 1):
                if b or c:
                    modes[(0, b, c)] = below[k][b][c] + above[k][b][c]
                modes[(1, b, c)] = above[k][b][c] - below[k][b][c]
        u.append(modes)
    unit = [(1, 0, 0), (0, 1, 0), (0, 0, 1)]

    def pair(i, j):
        return tuple(unit[i][d] + unit[j][d] for d in range(3))

    f = [{}, {}, {}]
    trace = (mod * (one * LAME)) * (u[0][unit[0]] + u[1][unit[1]] + u[2][unit[2]])
    stretch = mod * (2.0 * one * SHEAR)
    slide = mod * (one * SHEAR)
    for k in range(3):
        f[k][unit[k]] = trace + stretch * u[k][unit[k]]
    for i, j in ((0, 1), (1, 2), (0, 2)):
        shear = slide * (u[i][unit[j]] + u[j][unit[i]])
        f[i][unit[j]] = shear
        f[j][unit[i]] = shear
    same = mod * (two * (LAME + 3.0 * SHEAR))
    cross = mod * (two * LAME)
    for k in range(3):
        for m in range(3):
            if m != k:
                j = 3 - k - m
                f[k][pair(k, m)] = same * u[k][pair(k, m)] + cross * u[j][pair(j, m)]
    twist = mod * (two * SHEAR)
    total = u[0][pair(1, 2)] + u[1][pair(0, 2)] + u[2][pair(0, 1)]
    for k in range(3):
        i, j = [d for d in range(3) if d != k]
        f[k][pair(i, j)] = twist * (u[k][pair(i, j)] + total)
    warp = mod * (three * (LAME + 4.0 * SHEAR))
    for k in range(3):
        f[k][(1, 1, 1)] = warp * u[k][(1, 1, 1)]
    low = [[[None, None], [None, None]] for k in range(3)]
    high = [[[None, None], [None, None]] for k in range(3)]
    for k in range(3):
        for b in (0, 1):
            for c in (0, 1):
                if b or c:
                    low[k][b][c] = f[k][(0, b, c)] - f[k][(1, b, c)]
                    high[k][b][c] = f[k][(0, b, c)] + f[k][(1, b, c)]
                else:
                    low[k][b][c] = -f[k][(1, b, c)]
                    high[k][b][c] = f[k][(1, b, c)]
    return low, high


def plane_modes(value, ahead_y, ahead_x):
    shifted = ahead_x(value)
    rows = [value + shifted, shifted - value]
    out = [[None, None], [None, None]]
    for c in (0, 1):
        up = ahead_y(rows[c])
        out[0][c] = rows[c] + up
        out[1][c] = up - rows[c]
    return out


def plane_forces(force, behind_y, behind_x):
    rows = [
        (force[0][c] - force[1][c]) + behind_y(force[0][c] + force[1][c]) for c in (0, 1)
    ]
    return (rows[0] - rows[1]) + behind_x(rows[0] + rows[1])


def kernel(
    groups,
    members,
    load,
    phases,
    clamp,
    phase_moduli,
    out_u,
    out_r,
    R,
    LABEL,
    HELD,
    PART,
    SEAM,
    S,
    W,
    MOD,
    PH,
    FREE,
    PRO,
    ACC,
    STAGE,
    GAT,
    DOT,
    DSUM,
    DOTG,
    in_sem,
    halo_send,
    halo_recv,
    gat_send,
    gat_recv,
    cross_send,
    cross_recv,
    dot_send,
    dot_recv,
    dotg_send,
    dotg_recv,
):
    numbers = element_matrix()
    entry = float(numbers[0, 0])
    bound = spectral_bound(numbers)
    omega = 1.2 / bound
    _, layers, height, breadth = load.shape
    coarse_height = height // COARSEN
    coarse_breadth = breadth // COARSEN
    grp = lax.axis_index("grp")
    me = lax.axis_index("gz")
    tile = grp * members + me
    tiles = groups * members
    has_below = tile > 0
    has_above = tile < tiles - 1

    GAT[...] = jnp.zeros(GAT.shape, jnp.float32)
    barrier = pltpu.get_barrier_semaphore()

    def greet(to):
        pl.semaphore_signal(barrier, inc=1, device_id=to, device_id_type=MESH)

    def greet_member(o, unused):
        greet((grp, lax.rem(me + o, members)))
        return unused

    def greet_group(o, unused):
        greet((lax.rem(grp + o, groups), me))
        return unused

    lax.fori_loop(1, members, greet_member, 0)
    lax.fori_loop(1, groups, greet_group, 0)

    @pl.when((me == 0) & (grp > 0))
    def _():
        def greet_under(m, unused):
            greet((grp - 1, m))
            return unused

        lax.fori_loop(0, members, greet_under, 0)

    @pl.when((me == members - 1) & (grp < groups - 1))
    def _():
        def greet_over(m, unused):
            greet((grp + 1, m))
            return unused

        lax.fori_loop(0, members, greet_over, 0)

    greeted = (
        members - 1 + groups - 1 + jnp.where(grp > 0, 1, 0) + jnp.where(grp < groups - 1, 1, 0)
    )

    incoming = [
        pltpu.make_async_copy(load, R.at[0, :, HALO : HALO + layers], in_sem.at[0]),
        pltpu.make_async_copy(phases, LABEL, in_sem.at[1]),
        pltpu.make_async_copy(clamp, HELD, in_sem.at[2]),
    ]
    for copy in incoming:
        copy.start()

    @pl.when(tile == 0)
    def _():
        PH[0:3] = jnp.zeros((3, height, breadth), jnp.int32)
        for it in range(2):
            R[it, :, 0:HALO] = jnp.zeros((3, HALO, height, breadth), jnp.float32)

    @pl.when(tile == tiles - 1)
    def _():
        PH[3:5] = jnp.zeros((2, height, breadth), jnp.int32)
        for it in range(2):
            R[it, :, layers + HALO :] = jnp.zeros((3, HALO, height, breadth), jnp.float32)

    STAGE[...] = jnp.zeros(STAGE.shape, jnp.float32)
    for copy in incoming:
        copy.wait()
    first_depth = tile * layers
    bottom = jnp.where(tile == 0, 1.0, 0.0)
    free_plane = 1.0 - jnp.where(HELD[...] == 1, 1.0, 0.0) * bottom
    FREE[...] = free_plane
    for k in range(3):
        R[0, k, HALO] = free_plane * R[0, k, HALO]

    rows_at = lax.broadcasted_iota(jnp.int32, (height, breadth), 0)
    columns_at = lax.broadcasted_iota(jnp.int32, (height, breadth), 1)
    inside = (rows_at < height - 1) & (columns_at < breadth - 1)

    def moduli_of(labels, depth):
        picked = jnp.zeros((height, breadth), jnp.float32)
        for phase in range(PHASES):
            picked = jnp.where(labels == phase, phase_moduli[phase], picked)
        keep = jnp.where((depth >= 0) & (depth < tiles * layers - 1), 1.0, 0.0)
        return jnp.where(inside, picked, 0.0) * keep

    ACC[0] = jnp.zeros((height, breadth), jnp.float32)

    def own_layer(n, unused):
        mod = moduli_of(LABEL[n], first_depth + n)
        MOD[n + 3] = mod
        ACC[0] = ACC[0] + mod
        return unused

    lax.fori_loop(0, layers, own_layer, 0)

    def back_x(value):
        return pltpu.roll(value, 1, 1)

    def back_y(value):
        return pltpu.roll(value, 1, 0)

    def fore_x(value):
        return pltpu.roll(value, breadth - 1, 1)

    def inverse_layer(n, free):
        pair = MOD[n + 2] + MOD[n + 3]
        pair = pair + back_x(pair)
        pair = pair + back_y(pair)
        depth = first_depth + n
        valid = (depth >= 0) & (depth < tiles * layers)
        diagonal = entry * pair
        if free is not None:
            diagonal = free * diagonal + 1.0 - free
        W[n + HALO] = omega / jnp.where(valid, diagonal, 1.0)

    def inverse_inner(n, unused):
        inverse_layer(n, None)
        return unused

    lax.fori_loop(1, layers, inverse_inner, 0)

    pl.semaphore_wait(barrier, greeted)

    above_tile = jnp.minimum(tile + 1, tiles - 1)
    below_tile = jnp.maximum(tile - 1, 0)
    above_id = (above_tile // members, lax.rem(above_tile, members))
    below_id = (below_tile // members, lax.rem(below_tile, members))

    def to_above(src, dst, index):
        return pltpu.make_async_remote_copy(
            src_ref=src,
            dst_ref=dst,
            send_sem=halo_send.at[index],
            recv_sem=halo_recv.at[index],
            device_id=above_id,
            device_id_type=MESH,
        )

    def to_below(src, dst, index):
        return pltpu.make_async_remote_copy(
            src_ref=src,
            dst_ref=dst,
            send_sem=halo_send.at[index],
            recv_sem=halo_recv.at[index],
            device_id=below_id,
            device_id_type=MESH,
        )

    def field_up(it, depth):
        return to_above(
            R.at[it, :, HALO + layers - 1 - depth],
            R.at[it, :, HALO - 1 - depth],
            2 + it * 4 + depth,
        )

    def field_down(it, depth):
        return to_below(
            R.at[it, :, HALO + depth], R.at[it, :, HALO + layers + depth], 4 + it * 4 + depth
        )

    phases_up = to_above(LABEL.at[layers - 3 : layers], PH.at[0:3], 0)
    phases_down = to_below(LABEL.at[0:2], PH.at[3:5], 1)

    def start_field(it):
        for depth in range(HALO):

            @pl.when(has_above)
            def _():
                field_up(it, depth).start()

            @pl.when(has_below)
            def _():
                field_down(it, depth).start()

    def wait_field(it, depth):
        @pl.when(has_above)
        def _():
            field_up(it, depth).wait_send()
            field_down(it, depth).wait_recv()

        @pl.when(has_below)
        def _():
            field_down(it, depth).wait_send()
            field_up(it, depth).wait_recv()

    @pl.when(has_above)
    def _():
        phases_up.start()

    @pl.when(has_below)
    def _():
        phases_down.start()

    start_field(0)

    lanes = coarse_height * coarse_breadth
    fine_at = lax.broadcasted_iota(jnp.int32, (breadth, lanes), 0)
    lane_at = lax.broadcasted_iota(jnp.int32, (breadth, lanes), 1)
    gather_x = jnp.where(
        fine_at // COARSEN == lax.rem(lane_at, coarse_breadth), 1.0, 0.0
    ).astype(jnp.float32)
    coarse_at = lax.broadcasted_iota(jnp.int32, (lanes, breadth), 0)
    column_at = lax.broadcasted_iota(jnp.int32, (lanes, breadth), 1)
    spread_x = jnp.where(
        lax.rem(coarse_at, coarse_breadth) == column_at // COARSEN, 1.0, 0.0
    ).astype(jnp.float32)
    row_mask = jnp.where(
        lax.broadcasted_iota(jnp.int32, (coarse_height, lanes), 0)
        == lax.broadcasted_iota(jnp.int32, (coarse_height, lanes), 1) // coarse_breadth,
        1.0,
        0.0,
    ).astype(jnp.float32)

    def block_rows(planes):
        summed = [
            jnp.sum(plane.reshape(coarse_height, COARSEN, breadth), axis=1) for plane in planes
        ]
        wide = jnp.dot(
            jnp.concatenate(summed, 0),
            gather_x,
            precision=lax.Precision.HIGHEST,
            preferred_element_type=jnp.float32,
        )
        return [
            jnp.sum(
                wide[i * coarse_height : (i + 1) * coarse_height] * row_mask, axis=0, keepdims=True
            )
            for i in range(len(planes))
        ]

    def block_planes(rows):
        wide = jnp.concatenate(
            [jnp.broadcast_to(row, (coarse_height, lanes)) * row_mask for row in rows], 0
        )
        narrow = jnp.dot(
            wide, spread_x, precision=lax.Precision.HIGHEST, preferred_element_type=jnp.float32
        )
        return [
            jnp.broadcast_to(
                narrow[i * coarse_height : (i + 1) * coarse_height][:, None, :],
                (coarse_height, COARSEN, breadth),
            ).reshape(height, breadth)
            for i in range(len(rows))
        ]

    lane_row = lax.broadcasted_iota(jnp.int32, (1, lanes), 1)
    coarse_keep = (
        (lane_row // coarse_breadth < coarse_height - 1)
        & (lax.rem(lane_row, coarse_breadth) < coarse_breadth - 1)
    )
    in_group = jnp.where(me < members - 1, 1.0 / (COARSEN**3), 0.0)
    coarse_row = jnp.where(coarse_keep, block_rows([ACC[0]])[0], 0.0) * in_group
    for it in range(2):
        STAGE[it, 3:4] = coarse_row

    def halo_moduli():
        @pl.when(has_above)
        def _():
            phases_up.wait_send()
            phases_down.wait_recv()

        @pl.when(has_below)
        def _():
            phases_down.wait_send()
            phases_up.wait_recv()

        for n in range(3):
            MOD[n] = moduli_of(PH[n], first_depth - 3 + n)
        for n in range(2):
            MOD[layers + 3 + n] = moduli_of(PH[3 + n], first_depth + layers + n)
        for n in (-2, -1, 0, layers, layers + 1):
            inverse_layer(n, FREE[...] if n == 0 else None)

    chunks = height // 8
    row_at = lax.broadcasted_iota(jnp.int32, (8, breadth), 0)
    first_row = row_at == 0

    def sweep(get, put, start, stop, put_first=None, put_last=None):
        for n in range(start, stop + 1):
            for k in range(3):
                SEAM[n + HALO, k] = jnp.zeros((8, breadth), jnp.float32)

        def chunk(j, unused):
            rows = pl.ds(pl.multiple_of(j * 8, 8), 8)
            following_rows = pl.ds(pl.multiple_of(lax.rem(j + 1, chunks) * 8, 8), 8)

            def modes(n, masked):
                out = []
                for k in range(3):
                    here, after = get(k, n, rows), get(k, n, following_rows)
                    if masked:
                        here, after = FREE[rows] * here, FREE[following_rows] * after
                    over = pltpu.roll(jnp.where(first_row, after, here), 7, 0)
                    here_x, over_x = fore_x(here), fore_x(over)
                    sums = here + here_x, over + over_x
                    steps = here_x - here, over_x - over
                    out.append(
                        [
                            [sums[0] + sums[1], steps[0] + steps[1]],
                            [sums[1] - sums[0], steps[1] - steps[0]],
                        ]
                    )
                return out

            def emit(n, force, masked, to):
                for k in range(3):
                    e = [
                        (force[k][b][0] - force[k][b][1])
                        + back_x(force[k][b][0] + force[k][b][1])
                        for b in (0, 1)
                    ]
                    turned = pltpu.roll(e[0] + e[1], 1, 0)
                    total = (e[0] - e[1]) + jnp.where(first_row, SEAM[n + HALO, k], turned)
                    SEAM[n + HALO, k] = turned
                    if masked:
                        free = FREE[rows]
                        total = free * total + (1.0 - free) * get(k, n, rows)
                    to(k, n, rows, total)

            def step(v, below, carry, static):
                above = modes(v + 1, static and v + 1 == 0)
                low, high = voxel_forces(below, above, MOD[v + 3, rows], 1.0)
                if carry is None:
                    if put_first is not None:
                        emit(v, low, static and v == 0, put_first)
                else:
                    force = [
                        [[carry[k][b][c] + low[k][b][c] for c in (0, 1)] for b in (0, 1)]
                        for k in range(3)
                    ]
                    emit(v, force, static and v == 0, put)
                return above, high

            below, carry = modes(start, start == 0), None
            v = start
            while v < stop and (v <= max(start, 0)):
                below, carry = step(v, below, carry, True)
                v += 1
            if v < stop:

                def inner(at, state):
                    return step(at, state[0], state[1], False)

                below, carry = lax.fori_loop(v, stop, inner, (below, carry), unroll=True)
            if put_last is not None:
                emit(stop, carry, stop == 0, put_last)
            return unused

        lax.fori_loop(0, chunks, chunk, 0)

    def coarse_ahead(value, by):
        return pltpu.roll(value, lanes - by, 2)

    def coarse_behind(value, by):
        return pltpu.roll(value, by, 2)

    def coarse_apply(field, mod):
        fore = (
            functools.partial(coarse_ahead, by=coarse_breadth),
            functools.partial(coarse_ahead, by=1),
        )
        back = (
            functools.partial(coarse_behind, by=coarse_breadth),
            functools.partial(coarse_behind, by=1),
        )
        below = [plane_modes(field[k], *fore) for k in range(3)]
        above = [
            [[pltpu.roll(below[k][b][c], members - 1, 1) for c in (0, 1)] for b in (0, 1)]
            for k in range(3)
        ]
        low, high = voxel_forces(below, above, mod, float(COARSEN))
        out = []
        for k in range(3):
            force = [
                [low[k][b][c] + pltpu.roll(high[k][b][c], 1, 1) for c in (0, 1)] for b in (0, 1)
            ]
            out.append(plane_forces(force, *back))
        return out

    def coarse_solve(it):
        mod = GAT[it, :, :, 3, :]
        rhs = [GAT[it, :, :, k, :] for k in range(3)]
        pair = mod + pltpu.roll(mod, 1, 1)
        pair = pair + coarse_behind(pair, 1)
        pair = pair + coarse_behind(pair, coarse_breadth)
        diagonal = (COARSEN * entry) * pair
        present = diagonal > 0.0
        inverse = jnp.where(present, 1.0 / jnp.where(present, diagonal, 1.0), 0.0)
        low_end = bound / 20.0
        center = 0.5 * (bound + low_end)
        radius = 0.5 * (bound - low_end)
        sigma = center / radius
        rho = 1.0 / sigma
        update = [inverse * rhs[k] * (1.0 / center) for k in range(3)]
        correction = update
        remainder = rhs
        for sweep in range(CHEB - 1):
            image = coarse_apply(update, mod)
            remainder = [remainder[k] - image[k] for k in range(3)]
            rho_next = 1.0 / (2.0 * sigma - rho)
            update = [
                (rho_next * rho) * update[k] + (2.0 * rho_next / radius) * (inverse * remainder[k])
                for k in range(3)
            ]
            correction = [correction[k] + update[k] for k in range(3)]
            rho = rho_next
        return correction

    def peer_copy(it, o, src):
        other = lax.rem(me + o, members)
        return pltpu.make_async_remote_copy(
            src_ref=src,
            dst_ref=GAT.at[it, 0, me],
            send_sem=gat_send.at[it, o],
            recv_sem=gat_recv.at[it, me],
            device_id=(grp, other),
            device_id_type=MESH,
        )

    def peer_arrival(it, sender):
        return pltpu.make_async_remote_copy(
            src_ref=STAGE.at[it],
            dst_ref=GAT.at[it, 0, sender],
            send_sem=gat_send.at[it, 0],
            recv_sem=gat_recv.at[it, sender],
            device_id=(grp, sender),
            device_id_type=MESH,
        )

    def cross_copy(it, side, sender, target):
        return pltpu.make_async_remote_copy(
            src_ref=STAGE.at[it],
            dst_ref=GAT.at[it, 1, sender],
            send_sem=cross_send.at[it, side],
            recv_sem=cross_recv.at[it, sender],
            device_id=target,
            device_id_type=MESH,
        )

    under = (jnp.maximum(grp - 1, 0), members - 1)
    over = (jnp.minimum(grp + 1, groups - 1), 0)

    def gather_rows(it):
        def send(o, unused):
            peer_copy(it, o, STAGE.at[it]).start()
            return unused

        lax.fori_loop(1, members, send, 0)

        @pl.when(grp > 0)
        def _():
            cross_copy(it, 0, me, under).start()

        @pl.when(grp < groups - 1)
        def _():
            cross_copy(it, 1, me, over).start()

        GAT[it, 0, me] = STAGE[it]

        def arrive(o, unused):
            peer_copy(it, o, STAGE.at[it]).wait_send()
            peer_arrival(it, lax.rem(me + o, members)).wait_recv()
            return unused

        lax.fori_loop(1, members, arrive, 0)

        @pl.when(grp > 0)
        def _():
            cross_copy(it, 0, me, under).wait_send()

        @pl.when(grp < groups - 1)
        def _():
            cross_copy(it, 1, me, over).wait_send()

        @pl.when(((me == members - 1) & (grp < groups - 1)) | ((me == 0) & (grp > 0)))
        def _():
            def arrive_cross(sender, unused):
                cross_copy(it, 0, sender, under).wait_recv()
                return unused

            lax.fori_loop(0, members, arrive_cross, 0)

    for it in range(2):
        if it == 1:
            start_field(1)

        for k in range(3):
            ACC[k] = jnp.zeros((height, breadth), jnp.float32)

        def first_of(k, n, rows, it=it):
            return W[n + HALO, rows] * R[it, k, n + HALO, rows]

        def add_defect(k, n, rows, value, it=it):
            ACC[k, rows] = ACC[k, rows] + (R[it, k, n + HALO, rows] - value)

        def part(index):
            def to(k, n, rows, value):
                PART[index, k, rows] = value

            return to

        def with_part(index):
            def to(k, n, rows, value):
                add_defect(k, n, rows, PART[index, k, rows] + value)

            return to

        sweep(first_of, add_defect, 1, layers - 1, part(0), part(1))
        if it == 0:
            halo_moduli()
        wait_field(it, 0)
        sweep(first_of, add_defect, -1, 1, None, with_part(0))
        sweep(first_of, add_defect, layers - 1, layers, with_part(1), None)
        for k, row in enumerate(block_rows([ACC[k] for k in range(3)])):
            STAGE[it, k : k + 1] = row
        gather_rows(it)
        correction = coarse_solve(it)
        member_at = lax.broadcasted_iota(jnp.int32, (members, lanes), 0)

        def row_of(field, index):
            return jnp.sum(jnp.where(member_at == index, field, 0.0), axis=0, keepdims=True)

        spread_rows = []
        for k in range(3):
            own, other = correction[k][0], correction[k][1]
            spread_rows.append(
                jnp.where(me == 0, row_of(other, members - 1), row_of(own, me - 1))
            )
            spread_rows.append(row_of(own, me))
            spread_rows.append(
                jnp.where(me == members - 1, row_of(other, 0), row_of(own, me + 1))
            )
        for index, plane in enumerate(block_planes(spread_rows)):
            PRO[index % 3, index // 3] = plane

        wait_field(it, 1)

        def second_of(k, n, rows, it=it):
            block = jnp.where(n < 0, 0, jnp.where(n >= layers, 2, 1))
            spread = PRO[block, k, rows]
            if isinstance(n, int) and n == 0:
                spread = FREE[rows] * spread
            return first_of(k, n, rows, it) + spread

        def smooth(k, n, rows, value, it=it):
            S[it, k, n + HALO, rows] = second_of(k, n, rows, it) + W[n + HALO, rows] * (
                R[it, k, n + HALO, rows] - value
            )

        sweep(second_of, smooth, -2, layers + 1)

        def smoothed_of(k, n, rows, it=it):
            return S[it, k, n + HALO, rows]

        def keep_image(k, n, rows, value, it=it):
            R[it + 1, k, n + HALO, rows] = value

        sweep(smoothed_of, keep_image, -1, layers)

    ACC[...] = jnp.zeros(ACC.shape, jnp.float32)

    def products(n, unused):
        i = n + HALO
        for k in range(3):
            r, q, t = R[0, k, i], R[1, k, i], R[2, k, i]
            p, s = S[0, k, i], S[1, k, i]
            for index, value in enumerate((r * p, p * q, r * s, q * s, p * t, s * t)):
                ACC[index] = ACC[index] + value
        return unused

    lax.fori_loop(0, layers, products, 0)
    DSUM[...] = jnp.zeros(DSUM.shape, jnp.float32)
    for index in range(6):
        DSUM[0, index : index + 1] = jnp.sum(ACC[index], axis=0, keepdims=True)

    def dot_copy(o):
        return pltpu.make_async_remote_copy(
            src_ref=DSUM.at[0],
            dst_ref=DOT.at[me],
            send_sem=dot_send.at[o],
            recv_sem=dot_recv.at[me],
            device_id=(grp, lax.rem(me + o, members)),
            device_id_type=MESH,
        )

    def dot_arrival(sender):
        return pltpu.make_async_remote_copy(
            src_ref=DSUM.at[0],
            dst_ref=DOT.at[sender],
            send_sem=dot_send.at[0],
            recv_sem=dot_recv.at[sender],
            device_id=(grp, sender),
            device_id_type=MESH,
        )

    def dotg_copy(o):
        return pltpu.make_async_remote_copy(
            src_ref=DSUM.at[1],
            dst_ref=DOTG.at[grp],
            send_sem=dotg_send.at[o],
            recv_sem=dotg_recv.at[grp],
            device_id=(lax.rem(grp + o, groups), me),
            device_id_type=MESH,
        )

    def dotg_arrival(sender):
        return pltpu.make_async_remote_copy(
            src_ref=DSUM.at[1],
            dst_ref=DOTG.at[sender],
            send_sem=dotg_send.at[0],
            recv_sem=dotg_recv.at[sender],
            device_id=(sender, me),
            device_id_type=MESH,
        )

    def exchange(copy, arrival, own, size):
        def send(o, unused):
            copy(o).start()
            return unused

        def arrive(o, unused):
            copy(o).wait_send()
            arrival(lax.rem(own + o, size)).wait_recv()
            return unused

        lax.fori_loop(1, size, send, 0)
        return lambda: lax.fori_loop(1, size, arrive, 0)

    finish = exchange(dot_copy, dot_arrival, me, members)
    DOT[me] = DSUM[0]
    finish()
    DSUM[1] = jnp.sum(DOT[...], axis=0)
    finish = exchange(dotg_copy, dotg_arrival, grp, groups)
    DOTG[grp] = DSUM[1]
    finish()
    sums = jnp.sum(jnp.sum(DOTG[...], axis=0), axis=1, keepdims=True)
    rp, pq, rs, qs, pt, st = [sums[index : index + 1] for index in range(6)]
    alpha = rp / pq
    following = rp - alpha * (rs + pq) + alpha * alpha * qs
    curve = pq - alpha * (pt + qs) + alpha * alpha * st
    beta = following / rp
    alpha_two = following / (curve - beta * following / alpha)
    weight_a = alpha + alpha_two * (1.0 + beta)
    weight_b = alpha * alpha_two

    def finish_layer(n, unused):
        i = n + HALO
        for k in range(3):
            out_u[k, n] = weight_a * S[0, k, i] - weight_b * S[1, k, i]
            out_r[k, n] = R[0, k, i] - weight_a * R[1, k, i] + weight_b * R[2, k, i]
        return unused

    lax.fori_loop(0, layers, finish_layer, 0)


def body(groups, members, load, phases, clamp, phase_moduli):
    _, layers, height, breadth = load.shape
    assert layers == COARSEN
    plane = (height, breadth)
    deep = layers + 2 * HALO
    lanes = (height // COARSEN) * (breadth // COARSEN)
    vmem = pl.BlockSpec(memory_space=pltpu.VMEM)
    hbm = pl.BlockSpec(memory_space=pltpu.HBM)
    dma = pltpu.SemaphoreType.DMA
    f32 = jnp.float32
    return tuple(
        pl.pallas_call(
            functools.partial(kernel, groups, members),
            out_shape=(
                jax.ShapeDtypeStruct(load.shape, f32),
                jax.ShapeDtypeStruct(load.shape, f32),
            ),
            in_specs=[hbm, hbm, hbm, pl.BlockSpec(memory_space=pltpu.SMEM)],
            out_specs=(vmem, vmem),
            scratch_shapes=[
                pltpu.VMEM((3, 3, deep) + plane, f32),
                pltpu.VMEM((layers,) + plane, jnp.int32),
                pltpu.VMEM(plane, jnp.int32),
                pltpu.VMEM((2, 3) + plane, f32),
                pltpu.VMEM((deep, 3, 8, breadth), f32),
                pltpu.VMEM((2, 3, deep) + plane, f32),
                pltpu.VMEM((deep,) + plane, f32),
                pltpu.VMEM((deep + 1,) + plane, f32),
                pltpu.VMEM((5,) + plane, jnp.int32),
                pltpu.VMEM(plane, f32),
                pltpu.VMEM((3, 3) + plane, f32),
                pltpu.VMEM((6,) + plane, f32),
                pltpu.VMEM((2, 8, lanes), f32),
                pltpu.VMEM((2, 2, members, 8, lanes), f32),
                pltpu.VMEM((members, 8, breadth), f32),
                pltpu.VMEM((2, 8, breadth), f32),
                pltpu.VMEM((groups, 8, breadth), f32),
                dma((3,)),
                dma((10,)),
                dma((10,)),
                dma((2, members)),
                dma((2, members)),
                dma((2, 2)),
                dma((2, members)),
                dma((members,)),
                dma((members,)),
                dma((groups,)),
                dma((groups,)),
            ],
            compiler_params=pltpu.CompilerParams(
                collective_id=0, has_side_effects=True, vmem_limit_bytes=67043328
            ),
        )(load, phases, clamp, phase_moduli)
    )


def solution(mesh):
    groups, members = mesh.shape["grp"], mesh.shape["gz"]
    placed = (P(None, ("grp", "gz"), None, None), P(("grp", "gz"), None, None), P(), P())
    return jax.shard_map(
        functools.partial(body, groups, members),
        mesh=mesh,
        in_specs=placed,
        out_specs=(P(None, ("grp", "gz"), None, None), P(None, ("grp", "gz"), None, None)),
        check_vma=False,
    )
```
